32 devices in a mesh: ctx: 8 (over z, x), heads: 4 (over y, core).
Axes of the slice: x: 2, y: 2, z: 4, core: 2. Of those that a mesh axis runs over, the one named last changes fastest.
Arguments:
- queries: bfloat16 [64, 128, 576], P(None, 'heads'), may hold values from -60 to 60
- latents: bfloat16 [8192, 576], P('ctx'), may hold values from -6 to 6
- index_queries: bfloat16 [64, 64, 128], P(None, 'heads'), may hold values from -24 to 24
- index_keys: bfloat16 [8192, 128], P('ctx'), may hold values from -6 to 6
- index_weights: float32 [64, 64], P(None, 'heads'), may hold values from -15 to 15
- positions: int32 [64], replicated, may hold values from 2048 to 8191, as said below
Outputs:
- grad_index_queries: float32 [64, 64, 128], P(None, 'heads')
- grad_index_keys: float32 [8192, 128], P(('ctx', 'heads'))
The draws below stay inside these ranges and needn't reach their ends.
Inputs may be any that keep to these rules, and one draw needn't show every extreme that they name: Row q sees keys 0 to positions[q]. One row sits at 8191 and one at 2048.
All inputs are finite; a program needn't handle non-finite values.
Results may differ from the reference program's by a relative error of at most 0.0028.
Values sent between devices are 32-bit elements; how exact they have to be, the bound alone decides.
No kernel may reach another device: no remote copies, remote signals or barrier semaphores. Data moves between devices by JAX's collectives and lax.ppermute only.
A program may use at most 64 MiB of HBM per device.

```python
import jax
import jax.numpy as jnp
from jax import lax

Q = 64
KEY_DEV = 1024
H = 128
LAT = 576
HI = 64
DI = 128
TOKENS = 8192
LOSS_SCALE = 128


def main_pair(key):
    latent_values = jnp.clip(jax.random.normal(jax.random.fold_in(key, 101), (TOKENS, LAT), jnp.float32), -6.0, 6.0)
    query_values = jnp.clip(jax.random.normal(jax.random.fold_in(key, 102), (Q, H, LAT), jnp.float32), -6.0, 6.0)
    return (latent_values, query_values)


def index_triple(key):
    key_values = jnp.clip(jax.random.normal(jax.random.fold_in(key, 201), (TOKENS, DI), jnp.float32), -6.0, 6.0)
    query_values = jnp.clip(jax.random.normal(jax.random.fold_in(key, 202), (Q, HI, DI), jnp.float32), -6.0, 6.0)
    weight_values = jnp.clip(2.5 * jax.random.normal(jax.random.fold_in(key, 203), (Q, HI), jnp.float32), -15.0, 15.0)
    return (key_values, query_values, weight_values)


def draw_queries(key, part):
    return main_pair(key)[1].astype(jnp.bfloat16)


def draw_latents(key, part):
    return main_pair(key)[0].astype(jnp.bfloat16)


def draw_index_queries(key, part):
    return index_triple(key)[1].astype(jnp.bfloat16)


def draw_index_keys(key, part):
    return index_triple(key)[0].astype(jnp.bfloat16)


def draw_index_weights(key, part):
    return index_triple(key)[2].astype(jnp.float32)


def draw_positions(key, part):
    lowest = TOKENS // 4
    drawn = jax.random.randint(jax.random.fold_in(key, 301), (Q,), lowest, TOKENS)
    order = jax.random.permutation(jax.random.fold_in(key, 302), Q)
    drawn = drawn.at[order[0]].set(TOKENS - 1)
    drawn = drawn.at[order[1]].set(lowest)
    return drawn.astype(jnp.int32)


def setup_inputs(seed: int = 0) -> dict:
    splits = jax.random.split(jax.random.key(seed), 7)
    queries = draw_queries(jax.random.fold_in(splits[6], 71), 0)
    latents = draw_latents(jax.random.fold_in(splits[6], 71), 0)
    index_queries = draw_index_queries(jax.random.fold_in(splits[6], 71), 0)
    index_keys = draw_index_keys(jax.random.fold_in(splits[6], 71), 0)
    index_weights = draw_index_weights(jax.random.fold_in(splits[6], 71), 0)
    positions = draw_positions(jax.random.fold_in(splits[6], 71), 0)
    return dict(queries=queries, latents=latents, index_queries=index_queries, index_keys=index_keys, index_weights=index_weights, positions=positions)


score_scale = 192 ** -0.5
negative_fill = -1e30


def reference(queries, latents, index_queries, index_keys, index_weights, positions):
    nblocks = TOKENS // KEY_DEV
    flat_queries = queries.reshape(Q * H, LAT)
    flat_index = index_queries.reshape(Q * HI, DI)
    latent_blocks = latents.reshape(nblocks, KEY_DEV, LAT)
    key_blocks = index_keys.reshape(nblocks, KEY_DEV, DI)
    starts = jnp.arange(nblocks, dtype=jnp.int32) * KEY_DEV
    index_scale = (HI * DI) ** -0.5
    scaled_weights = index_weights * index_scale

    def block_view(offset):
        key_pos = offset + jnp.arange(KEY_DEV, dtype=jnp.int32)
        return key_pos[None, :] <= positions[:, None]

    def block_scores(latent_block, offset):
        products = jnp.dot(flat_queries, latent_block.T, preferred_element_type=jnp.float32)
        products = products.reshape(Q, H, KEY_DEV) * score_scale
        visible_now = block_view(offset)
        return jnp.where(visible_now[:, None, :], products, negative_fill), visible_now

    def first_step(running, inputs):
        run_max, run_total = running
        scores, visible_now = block_scores(inputs[0], inputs[1])
        new_max = jnp.maximum(run_max, jnp.max(scores, axis=2))
        added = jnp.sum(jnp.where(visible_now[:, None, :], jnp.exp(scores - new_max[:, :, None]), 0.0), axis=2)
        run_total = run_total * jnp.exp(run_max - new_max) + added
        return (new_max, run_total), None

    initial = (jnp.full((Q, H), negative_fill, jnp.float32), jnp.zeros((Q, H), jnp.float32))
    (row_max, row_total), ignored = lax.scan(first_step, initial, (latent_blocks, starts))

    def target_block(inputs):
        scores, visible_now = block_scores(inputs[0], inputs[1])
        weights_now = jnp.where(visible_now[:, None, :], jnp.exp(scores - row_max[:, :, None]) / row_total[:, :, None], 0.0)
        return jnp.sum(weights_now, axis=1)

    target = lax.map(target_block, (latent_blocks, starts))
    target = jnp.transpose(target, (1, 0, 2)).reshape(Q, TOKENS) * (1.0 / H)

    def index_dots(key_block):
        return jnp.dot(flat_index, key_block.T, preferred_element_type=jnp.float32).reshape(Q, HI, KEY_DEV)

    def logit_block(key_block):
        return jnp.sum(scaled_weights[:, :, None] * jnp.maximum(index_dots(key_block), 0.0), axis=1)

    logits = lax.map(logit_block, key_blocks)
    logits = jnp.transpose(logits, (1, 0, 2)).reshape(Q, TOKENS)
    visible_all = jnp.arange(TOKENS, dtype=jnp.int32)[None, :] <= positions[:, None]
    masked = jnp.where(visible_all, logits, negative_fill)
    row_peak = jnp.max(masked, axis=1)
    row_mass = jnp.sum(jnp.where(visible_all, jnp.exp(masked - row_peak[:, None]), 0.0), axis=1)
    index_probs = jnp.where(visible_all, jnp.exp(masked - row_peak[:, None]) / row_mass[:, None], 0.0)
    logit_grad = LOSS_SCALE * (index_probs - target)
    grad_blocks = jnp.transpose(logit_grad.reshape(Q, nblocks, KEY_DEV), (1, 0, 2))

    def back_step(running, inputs):
        key_block, grad_block = inputs
        dots_now = index_dots(key_block)
        coefficient = jnp.where(dots_now > 0.0, grad_block[:, None, :] * scaled_weights[:, :, None], 0.0)
        coefficient = coefficient.astype(jnp.bfloat16).reshape(Q * HI, KEY_DEV)
        running = running + jnp.dot(coefficient, key_block, preferred_element_type=jnp.float32)
        key_grad = lax.dot_general(coefficient, flat_index, (((0,), (0,)), ((), ())), preferred_element_type=jnp.float32)
        return running, key_grad

    grad_queries, grad_keys = lax.scan(back_step, jnp.zeros((Q * HI, DI), jnp.float32), (key_blocks, grad_blocks))
    return grad_queries.reshape(Q, HI, DI), grad_keys.reshape(TOKENS, DI)
```

```python
import functools
import math

import jax
import jax.numpy as jnp
from jax import lax
from jax.experimental import pallas as pl
from jax.experimental.pallas import tpu as pltpu
from jax.sharding import PartitionSpec as P

F32 = jnp.float32
BF16 = jnp.bfloat16
LOG2E = math.log2(math.e)
SCORE_LOG2 = 192 ** (-0.5) * LOG2E
NEG = -1e30
LANES = 128
VMEM = pl.BlockSpec(memory_space=pltpu.VMEM)
SMEM = pl.BlockSpec(memory_space=pltpu.SMEM)
CONTRACT_LAST = (((1,), (1,)), ((), ()))


def call(kernel, out_shape, n_smem, n_vmem, scratch=(), flops=0, exps=0, nbytes=0):
    outs = jax.tree.map(lambda s: VMEM, out_shape)
    return pl.pallas_call(
        kernel,
        out_shape=out_shape,
        in_specs=[SMEM] * n_smem + [VMEM] * n_vmem,
        out_specs=outs,
        scratch_shapes=list(scratch),
        compiler_params=pltpu.CompilerParams(vmem_limit_bytes=40 << 20),
        cost_estimate=pl.CostEstimate(flops=flops, transcendentals=exps, bytes_accessed=nbytes),
    )


def columns(ref_rows, count):
    padded = jnp.concatenate(
        [ref_rows, jnp.zeros((LANES - count, LANES), F32)], axis=0
    )
    return jnp.transpose(padded)


def logits_kernel(n_rows, n_heads, who_ref, iq_ref, ik_ref, iw_ref, keep_ref, send_ref, part):
    half = keep_ref.shape[1]
    wcol = columns(iw_ref[...], iw_ref.shape[0])
    rows = LANES
    per = rows // n_heads
    for b in range(n_rows * n_heads // rows):
        dots = lax.dot_general(
            iq_ref[b * rows : (b + 1) * rows, :], ik_ref[...], CONTRACT_LAST, preferred_element_type=F32
        )
        weighted = jnp.maximum(dots, 0.0) * wcol[:, b : b + 1]
        for i in range(per):
            part[b * per + i : b * per + i + 1, :] = jnp.sum(
                weighted[i * n_heads : (i + 1) * n_heads, :], axis=0, keepdims=True
            )
    core = who_ref[1]
    keep_ref[...] = part[:, pl.ds(pl.multiple_of(core * half, LANES), half)]
    send_ref[...] = part[:, pl.ds(pl.multiple_of((1 - core) * half, LANES), half)]


def scores_kernel(n_rows, n_heads, who_ref, pos_ref, q_ref, lat_ref, p_ref, stat_ref, s_even, s_odd, col):
    keys = lat_ref.shape[0]
    place = who_ref[0] + lax.broadcasted_iota(jnp.int32, (1, keys), 1)
    block = 256
    per = block // n_heads
    in_col = LANES // n_heads
    blocks = n_rows * n_heads // LANES
    col[...] = jnp.zeros_like(col)
    for b in range(n_rows * n_heads // block):
        held = s_even if b % 2 == 0 else s_odd
        held[...] = lax.dot_general(
            q_ref[b * block : (b + 1) * block, :], lat_ref[...], CONTRACT_LAST, preferred_element_type=F32
        )
        for i in range(per):
            row = b * per + i
            bias = jnp.where(place <= pos_ref[row], 0.0, NEG)
            x = held[i * n_heads : (i + 1) * n_heads, :] + bias
            top = jnp.max(x, axis=1, keepdims=True)
            e = jnp.exp2((x - top) * SCORE_LOG2)
            p_ref[row * n_heads : (row + 1) * n_heads, :] = e
            total = jnp.sum(e, axis=1, keepdims=True)
            lane = row // in_col
            at = (row % in_col) * n_heads
            col[at : at + n_heads, lane : lane + 1] = top
            col[at : at + n_heads, blocks + lane : blocks + lane + 1] = total
    stat_ref[...] = jnp.transpose(col[...])[: stat_ref.shape[0], :]


def index_stats_kernel(who_ref, pos_ref, mine_ref, other_ref, stat_ref, logit_ref, out_ref, col):
    n_rows, half = mine_ref.shape
    first = who_ref[0] + who_ref[1] * half
    place = first + lax.broadcasted_iota(jnp.int32, (1, half), 1)
    rows = lax.broadcasted_iota(jnp.int32, (n_rows, 1), 0)
    pos = jnp.zeros((n_rows, 1), jnp.int32)
    for r in range(n_rows):
        pos = jnp.where(rows == r, pos_ref[r], pos)
    x = jnp.where(place <= pos, (mine_ref[...] + other_ref[...]) * LOG2E, NEG)
    logit_ref[...] = x
    top = jnp.max(x, axis=1, keepdims=True)
    col[...] = jnp.zeros_like(col)
    col[:n_rows, 0:1] = top
    col[:n_rows, 1:2] = jnp.sum(jnp.exp2(x - top), axis=1, keepdims=True)
    n = stat_ref.shape[0]
    out_ref[:n, :] = stat_ref[...]
    out_ref[n:, :] = jnp.transpose(col[...])[: out_ref.shape[0] - n, :]


def joined(tops, totals, unit):
    top = tops[0]
    for t in tops[1:]:
        top = jnp.maximum(top, t)
    total = totals[0] * jnp.exp2((tops[0] - top) * unit)
    for t, l in zip(tops[1:], totals[1:]):
        total = total + l * jnp.exp2((t - top) * unit)
    return top, total


def target_kernel(n_rows, n_heads, who_ref, all_ref, own_ref, p_ref, keep_ref, send_ref, part):
    half = keep_ref.shape[1]
    n = all_ref.shape[0]
    blocks = n_rows * n_heads // LANES
    top, total = joined(
        [all_ref[k, :blocks, :] for k in range(n)],
        [all_ref[k, blocks : 2 * blocks, :] for k in range(n)],
        SCORE_LOG2,
    )
    weight = jnp.exp2((own_ref[:blocks, :] - top) * SCORE_LOG2) / total
    wcol = columns(weight, blocks)
    in_col = LANES // n_heads
    for row in range(n_rows):
        at = (row % in_col) * n_heads
        lane = row // in_col
        part[row : row + 1, :] = jnp.sum(
            p_ref[row * n_heads : (row + 1) * n_heads, :] * wcol[at : at + n_heads, lane : lane + 1],
            axis=0,
            keepdims=True,
        )
    peak, mass = joined(
        [all_ref[k, 2 * blocks : 2 * blocks + 1, :] for k in range(n)],
        [all_ref[k, 2 * blocks + 1 : 2 * blocks + 2, :] for k in range(n)],
        1.0,
    )
    core = who_ref[1]
    keep_ref[:n_rows, :] = part[:, pl.ds(pl.multiple_of(core * half, LANES), half)]
    send_ref[:n_rows, :] = part[:, pl.ds(pl.multiple_of((1 - core) * half, LANES), half)]
    stats = jnp.concatenate([peak, mass, jnp.zeros((6, LANES), F32)], axis=0)
    for ref in (keep_ref, send_ref):
        ref[n_rows:, :LANES] = stats
        ref[n_rows:, LANES:] = jnp.zeros((8, half - LANES), F32)


def probs_kernel(mine_ref, other_ref, logit_ref, prob_ref):
    n_rows = logit_ref.shape[0]
    peak, mass = joined(
        [mine_ref[n_rows : n_rows + 1, :LANES], other_ref[n_rows : n_rows + 1, :LANES]],
        [mine_ref[n_rows + 1 : n_rows + 2, :LANES], other_ref[n_rows + 1 : n_rows + 2, :LANES]],
        1.0,
    )
    stats = columns(jnp.concatenate([peak, 1.0 / mass], axis=0), 2)
    prob_ref[...] = jnp.exp2(logit_ref[...] - stats[:n_rows, 0:1]) * stats[:n_rows, 1:2]


def grads_kernel(n_rows, n_heads, who_ref, mine_ref, other_ref, iq_ref, ik_ref, iw_ref, gq_ref, *rest):
    *gk_refs, g_full, gk_t = rest
    half = mine_ref.shape[1]
    core = who_ref[1]
    g_full[:, pl.ds(pl.multiple_of(core * half, LANES), half)] = mine_ref[...]
    g_full[:, pl.ds(pl.multiple_of((1 - core) * half, LANES), half)] = other_ref[...]
    wcol = columns(iw_ref[...], iw_ref.shape[0])
    rows = LANES
    per = rows // n_heads
    blocks = n_rows * n_heads // rows
    for b in range(blocks):
        iq = iq_ref[b * rows : (b + 1) * rows, :]
        dots = lax.dot_general(iq, ik_ref[...], CONTRACT_LAST, preferred_element_type=F32)
        g = jnp.concatenate(
            [
                jnp.broadcast_to(g_full[b * per + i : b * per + i + 1, :], (n_heads, 2 * half))
                for i in range(per)
            ],
            axis=0,
        )
        coef = jnp.where(dots > 0.0, g * wcol[:, b : b + 1], 0.0).astype(BF16)
        gq_ref[b * rows : (b + 1) * rows, :] = jnp.dot(coef, ik_ref[...], preferred_element_type=F32)
        term = jnp.dot(jnp.transpose(iq), coef, preferred_element_type=F32)
        if b == 0:
            gk_t[...] = term
        else:
            gk_t[...] += term
    me = who_ref[2]
    size = gk_refs[0].shape[0]
    for k, ref in enumerate(gk_refs):
        at = pl.multiple_of((me ^ k) * size, LANES)
        ref[...] = jnp.transpose(gk_t[:, pl.ds(at, size)])


def body(queries, latents, index_queries, index_keys, index_weights, positions):
    n_rows, heads_local, width = queries.shape
    keys = latents.shape[0]
    index_local, depth = index_queries.shape[1:]
    n_ctx = lax.axis_size("ctx")
    n_heads = lax.axis_size("heads")
    half = keys // 2
    loss_scale = float(n_ctx * keys // 64)
    me = lax.axis_index("heads")
    who = jnp.stack([lax.axis_index("ctx") * keys, me % 2, me]).astype(jnp.int32)
    partner = [[(i, i ^ k) for i in range(n_heads)] for k in range(n_heads)]
    shape = jax.ShapeDtypeStruct
    iq = index_queries.reshape(n_rows * index_local, depth)
    weights = (index_weights * (index_local * n_heads * depth) ** (-0.5)).reshape(-1, LANES)

    def over_rest(value):
        k = 2
        while k < n_heads:
            value = value + lax.ppermute(value, "heads", partner[k])
            k *= 2
        return value

    keep, send = call(
        functools.partial(logits_kernel, n_rows, index_local),
        (shape((n_rows, half), F32),) * 2,
        1,
        3,
        [pltpu.VMEM((n_rows, keys), F32)],
        flops=2 * iq.size * keys,
        nbytes=keys * depth * 4,
    )(who, iq, index_keys, weights)
    logit_mine = keep + lax.ppermute(send, "heads", partner[1])
    logit_other = lax.ppermute(logit_mine, "heads", partner[2])

    stat_rows = 2 * n_rows * heads_local // LANES
    probs, stats = call(
        functools.partial(scores_kernel, n_rows, heads_local),
        (shape((n_rows * heads_local, keys), F32), shape((stat_rows, LANES), F32)),
        2,
        2,
        [pltpu.VMEM((256, keys), F32)] * 2 + [pltpu.VMEM((LANES, LANES), F32)],
        flops=2 * queries.size * keys,
        exps=n_rows * heads_local * keys,
        nbytes=queries.size * 2,
    )(who, positions, queries.reshape(n_rows * heads_local, width), latents)
    logits, stats = call(
        index_stats_kernel,
        (shape((n_rows, half), F32), shape((stat_rows + 8, LANES), F32)),
        2,
        3,
        [pltpu.VMEM((LANES, LANES), F32)],
    )(who, positions, logit_mine, logit_other, stats)
    everyone = lax.all_to_all(
        jnp.broadcast_to(stats, (n_ctx,) + stats.shape), "ctx", 0, 0
    )
    keep, send = call(
        functools.partial(target_kernel, n_rows, heads_local),
        (shape((n_rows + 8, half), F32),) * 2,
        1,
        3,
        [pltpu.VMEM((n_rows, keys), F32)],
    )(who, everyone, stats, probs)
    got = lax.ppermute(send, "heads", partner[1])
    index_probs = call(probs_kernel, shape((n_rows, half), F32), 0, 3)(keep, got, logits)
    target = over_rest(keep[:n_rows] + got[:n_rows])
    grad = loss_scale * (index_probs - target * (1.0 / (heads_local * n_heads)))
    grad_other = lax.ppermute(grad, "heads", partner[1])
    owned = keys // n_heads
    query_part, *key_parts = call(
        functools.partial(grads_kernel, n_rows, index_local),
        (shape((n_rows * index_local, depth), F32),) + (shape((owned, depth), F32),) * n_heads,
        1,
        5,
        [pltpu.VMEM((n_rows, keys), F32), pltpu.VMEM((depth, keys), F32)],
    )(who, grad, grad_other, iq, index_keys, weights)
    grad_keys = key_parts[0]
    for k in range(1, n_heads):
        grad_keys = grad_keys + lax.ppermute(key_parts[k], "heads", partner[k])
    blocks = query_part.reshape(n_ctx, -1, depth)
    mine = jnp.sum(lax.all_to_all(blocks, "ctx", 0, 0), axis=0)
    grad_queries = lax.all_to_all(jnp.broadcast_to(mine, blocks.shape), "ctx", 0, 0)
    return grad_queries.reshape(n_rows, index_local, depth), grad_keys


def solution(mesh):
    placed = (
        P(None, "heads", None),
        P("ctx", None),
        P(None, "heads", None),
        P("ctx", None),
        P(None, "heads"),
        P(),
    )
    return jax.shard_map(
        body,
        mesh=mesh,
        in_specs=placed,
        out_specs=(P(None, "heads", None), P(("ctx", "heads"), None)),
        check_vma=False,
    )
```

```python
import functools
import math

import jax
import jax.numpy as jnp
from jax import lax
from jax.experimental import pallas as pl
from jax.experimental.pallas import tpu as pltpu
from jax.sharding import PartitionSpec as P

F32 = jnp.float32
BF16 = jnp.bfloat16
LOG2E = math.log2(math.e)
SCORE_LOG2 = 192 ** (-0.5) * LOG2E
NEG = -1e30
LANES = 128
VMEM = pl.BlockSpec(memory_space=pltpu.VMEM)
SMEM = pl.BlockSpec(memory_space=pltpu.SMEM)
HBM = pl.BlockSpec(memory_space=pl.ANY)
CONTRACT_LAST = (((1,), (1,)), ((), ()))
QUAD = 4


def call(kernel, out_shape, in_specs, out_specs=None, scratch=(), flops=0, exps=0, nbytes=0):
    if out_specs is None:
        out_specs = jax.tree.map(lambda s: VMEM, out_shape)
    return pl.pallas_call(
        kernel,
        out_shape=out_shape,
        in_specs=in_specs,
        out_specs=out_specs,
        scratch_shapes=list(scratch),
        compiler_params=pltpu.CompilerParams(vmem_limit_bytes=40 << 20),
        cost_estimate=pl.CostEstimate(flops=flops, transcendentals=exps, bytes_accessed=nbytes),
    )


def half_at(core, half):
    return pl.ds(pl.multiple_of(core * half, LANES), half)


def logits_kernel(
    n_rows, n_heads, scale,
    pos_ref, iq_hbm, ik_hbm, iw_hbm, q_hbm, lat_hbm,
    keep_ref, send_ref, bias_ref, iq_ref, ik_ref, iw_ref, q_ref, lat_ref,
    part, sems,
):
    half = keep_ref.shape[1]
    copies = [
        pltpu.make_async_copy(a, b, sems.at[i])
        for i, (a, b) in enumerate(
            ((ik_hbm, ik_ref), (iq_hbm, iq_ref), (iw_hbm, iw_ref), (lat_hbm, lat_ref), (q_hbm, q_ref))
        )
    ]
    for copy in copies:
        copy.start()
    place = lax.axis_index("ctx") * 2 * half + lax.broadcasted_iota(jnp.int32, (1, 2 * half), 1)
    for row in range(n_rows):
        bias_ref[row : row + 1, :] = jnp.where(place <= pos_ref[row], 0.0, NEG)
    for copy in copies[:3]:
        copy.wait()
    iw_ref[...] = iw_ref[...] * scale
    rows = LANES
    per = rows // n_heads
    for b in range(n_rows * n_heads // rows):
        dots = lax.dot_general(
            iq_ref[b * rows : (b + 1) * rows, :], ik_ref[...], CONTRACT_LAST, preferred_element_type=F32
        )
        for i in range(per):
            row = b * per + i
            part[row : row + 1, :] = jnp.sum(
                jnp.maximum(dots[i * n_heads : (i + 1) * n_heads, :], 0.0) * iw_ref[:, row : row + 1],
                axis=0,
                keepdims=True,
            )
    core = lax.axis_index("heads") & 1
    mine, other = half_at(core, half), half_at(1 - core, half)
    keep_ref[...] = part[:, mine] + bias_ref[:, mine]
    send_ref[...] = part[:, other]
    for copy in copies[3:]:
        copy.wait()


def scores_kernel(n_rows, n_heads, bias_ref, q_ref, lat_ref, p_ref, stat_ref, s_even, s_odd):
    block = 256
    per = block // n_heads
    for b in range(n_rows * n_heads // block):
        held = s_even if b % 2 == 0 else s_odd
        held[...] = jnp.dot(
            q_ref[b * block : (b + 1) * block, :], lat_ref[...], preferred_element_type=F32
        )
        for i in range(per):
            row = b * per + i
            x = held[i * n_heads : (i + 1) * n_heads, :] + bias_ref[row : row + 1, :]
            top = jnp.max(x, axis=1, keepdims=True)
            e = jnp.exp2((x - top) * SCORE_LOG2)
            p_ref[row * n_heads : (row + 1) * n_heads, :] = e
            stat_ref[:, row : row + 1] = top
            stat_ref[:, n_rows + row : n_rows + row + 1] = jnp.sum(e, axis=1, keepdims=True)


def index_stats_kernel(mine_ref, other_ref, stat_ref, e_ref, out_ref, col):
    n_rows = mine_ref.shape[0]
    x = (mine_ref[...] + other_ref[...]) * LOG2E
    top = jnp.max(x, axis=1, keepdims=True)
    e = jnp.exp2(x - top)
    e_ref[...] = e
    col[:n_rows, 0:1] = top
    col[n_rows:, 0:1] = jnp.sum(e, axis=1, keepdims=True)
    n = stat_ref.shape[0]
    out_ref[:n, :] = stat_ref[...]
    out_ref[n:, :] = jnp.transpose(col[...])[: out_ref.shape[0] - n, :]


def joined(stats, unit):
    n = stats[0].shape[1] // 2
    tops = [s[:, :n] for s in stats]
    top = functools.reduce(jnp.maximum, tops)
    total = sum(s[:, n:] * jnp.exp2((t - top) * unit) for s, t in zip(stats, tops))
    return top, total


def target_kernel(n_rows, n_heads, all_ref, own_ref, p_ref, keep_ref, send_ref, part):
    half = keep_ref.shape[1]
    n = all_ref.shape[0]
    top, total = joined([all_ref[k, :n_heads, :] for k in range(n)], SCORE_LOG2)
    weight = jnp.exp2((own_ref[:n_heads, :n_rows] - top) * SCORE_LOG2) / total
    for row in range(n_rows):
        part[row : row + 1, :] = jnp.sum(
            p_ref[row * n_heads : (row + 1) * n_heads, :] * weight[:, row : row + 1],
            axis=0,
            keepdims=True,
        )
    peak, mass = joined([all_ref[k, n_heads:, :] for k in range(n)], 1.0)
    core = lax.axis_index("heads") & 1
    keep_ref[:n_rows, :] = part[:, half_at(core, half)]
    send_ref[:n_rows, :] = part[:, half_at(1 - core, half)]
    for ref in (keep_ref, send_ref):
        ref[n_rows:, :n_rows] = peak
        ref[n_rows:, n_rows : 2 * n_rows] = mass


def probs_kernel(mine_ref, other_ref, own_ref, e_ref, prob_ref, col):
    n_rows = e_ref.shape[0]
    peak, mass = joined([ref[n_rows:, : 2 * n_rows] for ref in (mine_ref, other_ref)], 1.0)
    factor = jnp.exp2(own_ref[own_ref.shape[0] - 8 :, :n_rows] - peak) / mass
    col[:8, :n_rows] = factor
    prob_ref[...] = e_ref[...] * jnp.transpose(col[...])[:n_rows, 0:1]


def grads_kernel(n_rows, n_heads, mine_ref, other_ref, iq_ref, ik_ref, iw_ref, *rest):
    *out_refs, g_full, gk_t, w_cols = rest
    gq_refs, gk_refs = out_refs[:QUAD], out_refs[QUAD:]
    half = mine_ref.shape[1]
    me = lax.axis_index("heads")
    core = me & 1
    g_full[:, half_at(core, half)] = mine_ref[...]
    g_full[:, half_at(1 - core, half)] = other_ref[...]
    for row in range(n_rows):
        w_cols[row * n_heads : (row + 1) * n_heads, :] = jnp.broadcast_to(
            iw_ref[:, row : row + 1], (n_heads, LANES)
        )
    slot = lax.axis_index("ctx") & (QUAD - 1)
    rows = LANES
    per = rows // n_heads
    size = n_rows // QUAD
    for k in range(QUAD):
        for b in range(size // per):
            first = pl.multiple_of((slot ^ k) * size, size) + b * per
            at = pl.ds(pl.multiple_of(first * n_heads, rows), rows)
            iq = iq_ref[at, :]
            dots = lax.dot_general(iq, ik_ref[...], CONTRACT_LAST, preferred_element_type=F32)
            g_rows = g_full[pl.ds(pl.multiple_of(first, per), per), :]
            g = jnp.concatenate(
                [jnp.broadcast_to(g_rows[i : i + 1, :], (n_heads, 2 * half)) for i in range(per)], axis=0
            )
            coef = jnp.where(dots > 0.0, g * w_cols[at, 0:1], 0.0).astype(BF16)
            gq_refs[k][b * rows : (b + 1) * rows, :] = jnp.dot(
                coef, ik_ref[...], preferred_element_type=F32
            )
            term = jnp.dot(jnp.transpose(iq), coef, preferred_element_type=F32)
            if k == 0 and b == 0:
                gk_t[...] = term
            else:
                gk_t[...] += term
    size = gk_refs[0].shape[0]
    for k, ref in enumerate(gk_refs):
        at = pl.multiple_of((me ^ k) * size, LANES)
        ref[...] = jnp.transpose(gk_t[:, pl.ds(at, size)])


def outputs_kernel(n_quad, *refs):
    *in_refs, gq_hbm, gk_hbm, total, sems = refs
    blocks, parts = in_refs[:n_quad], in_refs[n_quad:]
    size = blocks[0].shape[0]
    slot = lax.axis_index("ctx") & (n_quad - 1)
    copies = [
        pltpu.make_async_copy(
            ref, gq_hbm.at[pl.ds(pl.multiple_of((slot ^ k) * size, size), size), :], sems.at[k]
        )
        for k, ref in enumerate(blocks)
    ]
    for copy in copies:
        copy.start()
    total[...] = sum(ref[...] for ref in parts)
    last = pltpu.make_async_copy(total, gk_hbm, sems.at[n_quad])
    last.start()
    for copy in copies + [last]:
        copy.wait()


def body(queries, latents, index_queries, index_keys, index_weights, positions):
    n_rows, heads_local, width = queries.shape
    keys = latents.shape[0]
    index_local, depth = index_queries.shape[1:]
    n_ctx = lax.axis_size("ctx")
    n_heads = lax.axis_size("heads")
    half = keys // 2
    loss_scale = float(n_ctx * keys // 64)
    shape = jax.ShapeDtypeStruct

    def swapped(value, axis, k):
        n = lax.axis_size(axis)
        return lax.ppermute(value, axis, [(i, i ^ k) for i in range(n)])

    flat = (n_rows * index_local, depth)
    keep, send, bias, iq, ik, iw, q, lat = call(
        functools.partial(
            logits_kernel, n_rows, index_local, (index_local * n_heads * depth) ** (-0.5)
        ),
        (
            shape((n_rows, half), F32),
            shape((n_rows, half), F32),
            shape((n_rows, keys), F32),
            shape(flat, BF16),
            shape((keys, depth), BF16),
            shape((index_local, n_rows), F32),
            shape((n_rows * heads_local, width), BF16),
            shape((width, keys), BF16),
        ),
        [SMEM] + [HBM] * 5,
        scratch=[pltpu.VMEM((n_rows, keys), F32), pltpu.SemaphoreType.DMA((5,))],
        flops=2 * flat[0] * depth * keys,
        nbytes=queries.size * 2 + latents.size * 2,
    )(
        positions,
        index_queries.reshape(flat),
        index_keys,
        index_weights.T,
        queries.reshape(n_rows * heads_local, width),
        latents.T,
    )
    logit_mine = keep + swapped(send, "heads", 1)
    logit_other = swapped(logit_mine, "heads", 2)
    probs, stats = call(
        functools.partial(scores_kernel, n_rows, heads_local),
        (shape((n_rows * heads_local, keys), F32), shape((heads_local, 2 * n_rows), F32)),
        [VMEM] * 3,
        scratch=[pltpu.VMEM((256, keys), F32)] * 2,
        flops=2 * queries.size * keys,
        exps=n_rows * heads_local * keys,
        nbytes=queries.size * 2,
    )(bias, q, lat)
    exps, stats = call(
        index_stats_kernel,
        (shape((n_rows, half), F32), shape((heads_local + 8, 2 * n_rows), F32)),
        [VMEM] * 3,
        scratch=[pltpu.VMEM((LANES, LANES), F32)],
    )(logit_mine, logit_other, stats)
    everyone = lax.all_to_all(jnp.broadcast_to(stats, (n_ctx,) + stats.shape), "ctx", 0, 0)
    keep, send = call(
        functools.partial(target_kernel, n_rows, heads_local),
        (shape((n_rows + 8, half), F32),) * 2,
        [VMEM] * 3,
        scratch=[pltpu.VMEM((n_rows, keys), F32)],
    )(everyone, stats, probs)
    got = swapped(send, "heads", 1)
    index_probs = call(
        probs_kernel,
        shape((n_rows, half), F32),
        [VMEM] * 4,
        scratch=[pltpu.VMEM((LANES, LANES), F32)],
    )(keep, got, stats, exps)
    target = keep[:n_rows] + got[:n_rows]
    target = target + swapped(target, "heads", 2)
    grad = loss_scale * (index_probs - target * (1.0 / (heads_local * n_heads)))
    grad_other = swapped(grad, "heads", 1)
    owned = keys // n_heads
    block = (flat[0] // QUAD, depth)
    parts = call(
        functools.partial(grads_kernel, n_rows, index_local),
        (shape(block, F32),) * QUAD + (shape((owned, depth), F32),) * n_heads,
        [VMEM] * 5,
        scratch=[
            pltpu.VMEM((n_rows, keys), F32),
            pltpu.VMEM((depth, keys), F32),
            pltpu.VMEM((flat[0], LANES), F32),
        ],
    )(grad, grad_other, iq, ik, iw)
    query_parts, key_parts = parts[:QUAD], parts[QUAD:]
    mine = query_parts[0] + sum(swapped(query_parts[k], "ctx", k) for k in range(1, QUAD))
    key_parts = [key_parts[0]] + [swapped(key_parts[k], "heads", k) for k in range(1, n_heads)]
    k = QUAD
    while k < n_ctx:
        mine = mine + swapped(mine, "ctx", k)
        k *= 2
    blocks = [mine] + [swapped(mine, "ctx", k) for k in range(1, QUAD)]
    grad_queries, grad_keys = call(
        functools.partial(outputs_kernel, QUAD),
        (shape(flat, F32), shape((owned, depth), F32)),
        [VMEM] * (QUAD + n_heads),
        out_specs=(HBM, HBM),
        scratch=[pltpu.VMEM((owned, depth), F32), pltpu.SemaphoreType.DMA((QUAD + 1,))],
    )(*blocks, *key_parts)
    return grad_queries.reshape(n_rows, index_local, depth), grad_keys


def solution(mesh):
    placed = (
        P(None, "heads", None),
        P("ctx", None),
        P(None, "heads", None),
        P("ctx", None),
        P(None, "heads"),
        P(),
    )
    return jax.shard_map(
        body,
        mesh=mesh,
        in_specs=placed,
        out_specs=(P(None, "heads", None), P(("ctx", "heads"), None)),
        check_vma=False,
    )
```

```python
import functools
import math

import jax
import jax.numpy as jnp
from jax import lax
from jax.experimental import pallas as pl
from jax.experimental.pallas import tpu as pltpu
from jax.sharding import PartitionSpec as P

F32 = jnp.float32
BF16 = jnp.bfloat16
LOG2E = math.log2(math.e)
SCORE_LOG2 = 192 ** (-0.5) * LOG2E
NEG = -1e30
LANES = 128
VMEM = pl.BlockSpec(memory_space=pltpu.VMEM)
HBM = pl.BlockSpec(memory_space=pltpu.HBM)
CONTRACT_LAST = (((1,), (1,)), ((), ()))
COLUMNS = 256
QUAD = 4


def call(kernel, out_shape, in_specs, out_specs=None, scratch=(), flops=0, exps=0, nbytes=0):
    if out_specs is None:
        out_specs = jax.tree.map(lambda s: VMEM, out_shape)
    return pl.pallas_call(
        kernel,
        out_shape=out_shape,
        in_specs=in_specs,
        out_specs=out_specs,
        scratch_shapes=list(scratch),
        compiler_params=pltpu.CompilerParams(vmem_limit_bytes=40 << 20),
        cost_estimate=pl.CostEstimate(flops=flops, transcendentals=exps, bytes_accessed=nbytes),
    )


def half_at(core, half):
    return pl.ds(pl.multiple_of(core * half, LANES), half)


def logits_kernel(
    n_rows, n_heads, scale,
    pos_hbm, iq_hbm, ik_hbm, iw_hbm, q_hbm, lat_hbm,
    keep_ref, send_ref, bias_ref, iq_ref, ik_ref, iw_ref, q_ref, lat_ref,
    part, pos_ref, sems,
):
    half = keep_ref.shape[1]
    copies = [
        pltpu.make_async_copy(a, b, sems.at[i])
        for i, (a, b) in enumerate(
            (
                (pos_hbm, pos_ref),
                (ik_hbm, ik_ref),
                (iq_hbm, iq_ref),
                (iw_hbm, iw_ref),
                (lat_hbm, lat_ref),
                (q_hbm, q_ref),
            )
        )
    ]
    for copy in copies:
        copy.start()
    copies[0].wait()
    place = lax.axis_index("ctx") * 2 * half + lax.broadcasted_iota(jnp.int32, (1, 2 * half), 1)
    for row in range(n_rows):
        bias_ref[row : row + 1, :] = jnp.where(place <= pos_ref[row], 0.0, NEG)
    for copy in copies[1:4]:
        copy.wait()
    iw_ref[...] = iw_ref[...] * scale
    rows = LANES
    per = rows // n_heads
    for b in range(n_rows * n_heads // rows):
        dots = lax.dot_general(
            iq_ref[b * rows : (b + 1) * rows, :], ik_ref[...], CONTRACT_LAST, preferred_element_type=F32
        )
        for i in range(per):
            row = b * per + i
            part[row : row + 1, :] = jnp.sum(
                jnp.maximum(dots[i * n_heads : (i + 1) * n_heads, :], 0.0) * iw_ref[:, row : row + 1],
                axis=0,
                keepdims=True,
            )
    core = lax.axis_index("heads") & 1
    mine, other = half_at(core, half), half_at(1 - core, half)
    keep_ref[...] = part[:, mine] + bias_ref[:, mine]
    send_ref[...] = part[:, other]
    for copy in copies[4:]:
        copy.wait()


def scores_kernel(n_rows, n_heads, bias_ref, q_ref, lat_ref, p_ref, stat_ref, s_even, s_odd):
    block = s_even.shape[0]
    keys = lat_ref.shape[1]
    steps = keys // COLUMNS
    per = block // n_heads // steps
    strips = n_rows * n_heads // block * steps
    for step in range(strips + steps):
        if step < strips:
            b, n = divmod(step, steps)
            held = s_even if b % 2 == 0 else s_odd
            held[:, n * COLUMNS : (n + 1) * COLUMNS] = jnp.dot(
                q_ref[b * block : (b + 1) * block, :],
                lat_ref[:, n * COLUMNS : (n + 1) * COLUMNS],
                preferred_element_type=F32,
            )
        if step >= steps:
            b, n = divmod(step - steps, steps)
            held = s_even if b % 2 == 0 else s_odd
            for i in range(n * per, (n + 1) * per):
                row = b * (block // n_heads) + i
                x = held[i * n_heads : (i + 1) * n_heads, :] + bias_ref[row : row + 1, :]
                top = jnp.max(x, axis=1, keepdims=True)
                e = jnp.exp2((x - top) * SCORE_LOG2)
                p_ref[row * n_heads : (row + 1) * n_heads, :] = e
                stat_ref[:, row : row + 1] = top
                stat_ref[:, n_rows + row : n_rows + row + 1] = jnp.sum(e, axis=1, keepdims=True)


def index_stats_kernel(mine_ref, other_ref, stat_ref, e_ref, out_ref, col):
    n_rows = mine_ref.shape[0]
    x = (mine_ref[...] + other_ref[...]) * LOG2E
    top = jnp.max(x, axis=1, keepdims=True)
    e = jnp.exp2(x - top)
    e_ref[...] = e
    col[:n_rows, 0:1] = top
    col[n_rows:, 0:1] = jnp.sum(e, axis=1, keepdims=True)
    n = stat_ref.shape[0]
    out_ref[:n, :] = stat_ref[...]
    out_ref[n:, :] = jnp.transpose(col[...])[: out_ref.shape[0] - n, :]


def joined(stats, unit):
    n = stats[0].shape[1] // 2
    tops = [s[:, :n] for s in stats]
    top = functools.reduce(jnp.maximum, tops)
    total = sum(s[:, n:] * jnp.exp2((t - top) * unit) for s, t in zip(stats, tops))
    return top, total


def target_kernel(n_rows, n_heads, all_ref, own_ref, p_ref, keep_ref, send_ref, part):
    half = keep_ref.shape[1]
    n = all_ref.shape[0]
    top, total = joined([all_ref[k, :n_heads, :] for k in range(n)], SCORE_LOG2)
    weight = jnp.exp2((own_ref[:n_heads, :n_rows] - top) * SCORE_LOG2) / total
    for row in range(n_rows):
        part[row : row + 1, :] = jnp.sum(
            p_ref[row * n_heads : (row + 1) * n_heads, :] * weight[:, row : row + 1],
            axis=0,
            keepdims=True,
        )
    peak, mass = joined([all_ref[k, n_heads:, :] for k in range(n)], 1.0)
    core = lax.axis_index("heads") & 1
    keep_ref[:n_rows, :] = part[:, half_at(core, half)]
    send_ref[:n_rows, :] = part[:, half_at(1 - core, half)]
    for ref in (keep_ref, send_ref):
        ref[n_rows:, :n_rows] = peak
        ref[n_rows:, n_rows : 2 * n_rows] = mass


def probs_kernel(mine_ref, other_ref, own_ref, e_ref, prob_ref, col):
    n_rows = e_ref.shape[0]
    peak, mass = joined([ref[n_rows:, : 2 * n_rows] for ref in (mine_ref, other_ref)], 1.0)
    factor = jnp.exp2(own_ref[own_ref.shape[0] - 8 :, :n_rows] - peak) / mass
    col[:8, :n_rows] = factor
    prob_ref[...] = e_ref[...] * jnp.transpose(col[...])[:n_rows, 0:1]


def grads_kernel(n_rows, n_heads, mine_ref, other_ref, iq_ref, ik_ref, iw_ref, *rest):
    *out_refs, g_full, gk_t, w_cols = rest
    gq_refs, gk_refs = out_refs[:QUAD], out_refs[QUAD:]
    half = mine_ref.shape[1]
    me = lax.axis_index("heads")
    core = me & 1
    g_full[:, half_at(core, half)] = mine_ref[...]
    g_full[:, half_at(1 - core, half)] = other_ref[...]
    for row in range(n_rows):
        w_cols[row * n_heads : (row + 1) * n_heads, :] = jnp.broadcast_to(
            iw_ref[:, row : row + 1], (n_heads, LANES)
        )
    slot = lax.axis_index("ctx") & (QUAD - 1)
    rows = LANES
    per = rows // n_heads
    size = n_rows // QUAD
    for k in range(QUAD):
        for b in range(size // per):
            first = pl.multiple_of((slot ^ k) * size, size) + b * per
            at = pl.ds(pl.multiple_of(first * n_heads, rows), rows)
            iq = iq_ref[at, :]
            dots = lax.dot_general(iq, ik_ref[...], CONTRACT_LAST, preferred_element_type=F32)
            g_rows = g_full[pl.ds(pl.multiple_of(first, per), per), :]
            g = jnp.concatenate(
                [jnp.broadcast_to(g_rows[i : i + 1, :], (n_heads, 2 * half)) for i in range(per)], axis=0
            )
            coef = jnp.where(dots > 0.0, g * w_cols[at, 0:1], 0.0).astype(BF16)
            gq_refs[k][b * rows : (b + 1) * rows, :] = jnp.dot(
                coef, ik_ref[...], preferred_element_type=F32
            )
            term = jnp.dot(jnp.transpose(iq), coef, preferred_element_type=F32)
            if k == 0 and b == 0:
                gk_t[...] = term
            else:
                gk_t[...] += term
    size = gk_refs[0].shape[0]
    for k, ref in enumerate(gk_refs):
        at = pl.multiple_of((me ^ k) * size, LANES)
        ref[...] = jnp.transpose(gk_t[:, pl.ds(at, size)])


def outputs_kernel(n_quad, *refs):
    *in_refs, gq_hbm, gk_hbm, total, sems = refs
    blocks, parts = in_refs[:n_quad], in_refs[n_quad:]
    size = blocks[0].shape[0]
    slot = lax.axis_index("ctx") & (n_quad - 1)
    copies = [
        pltpu.make_async_copy(
            ref, gq_hbm.at[pl.ds(pl.multiple_of((slot ^ k) * size, size), size), :], sems.at[k]
        )
        for k, ref in enumerate(blocks)
    ]
    for copy in copies:
        copy.start()
    total[...] = sum(ref[...] for ref in parts)
    last = pltpu.make_async_copy(total, gk_hbm, sems.at[n_quad])
    last.start()
    for copy in copies + [last]:
        copy.wait()


def body(queries, latents, index_queries, index_keys, index_weights, positions):
    n_rows, heads_local, width = queries.shape
    keys = latents.shape[0]
    index_local, depth = index_queries.shape[1:]
    n_ctx = lax.axis_size("ctx")
    n_heads = lax.axis_size("heads")
    half = keys // 2
    loss_scale = float(n_ctx * keys // 64)
    shape = jax.ShapeDtypeStruct

    def swapped(value, axis, k):
        n = lax.axis_size(axis)
        return lax.ppermute(value, axis, [(i, i ^ k) for i in range(n)])

    flat = (n_rows * index_local, depth)
    keep, send, bias, iq, ik, iw, q, lat = call(
        functools.partial(
            logits_kernel, n_rows, index_local, (index_local * n_heads * depth) ** (-0.5)
        ),
        (
            shape((n_rows, half), F32),
            shape((n_rows, half), F32),
            shape((n_rows, keys), F32),
            shape(flat, BF16),
            shape((keys, depth), BF16),
            shape((index_local, n_rows), F32),
            shape((n_rows * heads_local, width), BF16),
            shape((width, keys), BF16),
        ),
        [HBM] * 6,
        scratch=[
            pltpu.VMEM((n_rows, keys), F32),
            pltpu.SMEM((n_rows,), jnp.int32),
            pltpu.SemaphoreType.DMA((6,)),
        ],
        flops=2 * flat[0] * depth * keys,
        nbytes=queries.size * 2 + latents.size * 2,
    )(
        *(
            pltpu.with_memory_space_constraint(x, pltpu.HBM)
            for x in (
                positions,
                index_queries.reshape(flat),
                index_keys,
                index_weights.T,
                queries.reshape(n_rows * heads_local, width),
                latents.T,
            )
        ),
    )
    logit_mine = keep + swapped(send, "heads", 1)
    logit_other = swapped(logit_mine, "heads", 2)
    probs, stats = call(
        functools.partial(scores_kernel, n_rows, heads_local),
        (shape((n_rows * heads_local, keys), F32), shape((heads_local, 2 * n_rows), F32)),
        [VMEM] * 3,
        scratch=[pltpu.VMEM((256, keys), F32)] * 2,
        flops=2 * queries.size * keys,
        exps=n_rows * heads_local * keys,
        nbytes=queries.size * 2,
    )(bias, q, lat)
    exps, stats = call(
        index_stats_kernel,
        (shape((n_rows, half), F32), shape((heads_local + 8, 2 * n_rows), F32)),
        [VMEM] * 3,
        scratch=[pltpu.VMEM((LANES, LANES), F32)],
    )(logit_mine, logit_other, stats)
    everyone = lax.all_to_all(jnp.broadcast_to(stats, (n_ctx,) + stats.shape), "ctx", 0, 0)
    keep, send = call(
        functools.partial(target_kernel, n_rows, heads_local),
        (shape((n_rows + 8, half), F32),) * 2,
        [VMEM] * 3,
        scratch=[pltpu.VMEM((n_rows, keys), F32)],
    )(everyone, stats, probs)
    got = swapped(send, "heads", 1)
    index_probs = call(
        probs_kernel,
        shape((n_rows, half), F32),
        [VMEM] * 4,
        scratch=[pltpu.VMEM((LANES, LANES), F32)],
    )(keep, got, stats, exps)
    target = keep[:n_rows] + got[:n_rows]
    target = target + swapped(target, "heads", 2)
    grad = loss_scale * (index_probs - target * (1.0 / (heads_local * n_heads)))
    grad_other = swapped(grad, "heads", 1)
    owned = keys // n_heads
    block = (flat[0] // QUAD, depth)
    parts = call(
        functools.partial(grads_kernel, n_rows, index_local),
        (shape(block, F32),) * QUAD + (shape((owned, depth), F32),) * n_heads,
        [VMEM] * 5,
        scratch=[
            pltpu.VMEM((n_rows, keys), F32),
            pltpu.VMEM((depth, keys), F32),
            pltpu.VMEM((flat[0], LANES), F32),
        ],
    )(grad, grad_other, iq, ik, iw)
    query_parts, key_parts = parts[:QUAD], parts[QUAD:]
    mine = query_parts[0] + sum(swapped(query_parts[k], "ctx", k) for k in range(1, QUAD))
    key_parts = [key_parts[0]] + [swapped(key_parts[k], "heads", k) for k in range(1, n_heads)]
    k = QUAD
    while k < n_ctx:
        mine = mine + swapped(mine, "ctx", k)
        k *= 2
    blocks = [mine] + [swapped(mine, "ctx", k) for k in range(1, QUAD)]
    grad_queries, grad_keys = call(
        functools.partial(outputs_kernel, QUAD),
        (shape(flat, F32), shape((owned, depth), F32)),
        [VMEM] * (QUAD + n_heads),
        out_specs=(HBM, HBM),
        scratch=[pltpu.VMEM((owned, depth), F32), pltpu.SemaphoreType.DMA((QUAD + 1,))],
    )(*blocks, *key_parts)
    return grad_queries.reshape(n_rows, index_local, depth), grad_keys


def solution(mesh):
    placed = (
        P(None, "heads", None),
        P("ctx", None),
        P(None, "heads", None),
        P("ctx", None),
        P(None, "heads"),
        P(),
    )
    return jax.shard_map(
        body,
        mesh=mesh,
        in_specs=placed,
        out_specs=(P(None, "heads", None), P(("ctx", "heads"), None)),
        check_vma=False,
    )
```

```python
import functools
import math

import jax
import jax.numpy as jnp
from jax import lax
from jax.experimental import pallas as pl
from jax.experimental.pallas import tpu as pltpu
from jax.sharding import PartitionSpec as P


F32 = jnp.float32
BF16 = jnp.bfloat16
LOG2E = math.log2(math.e)
SCORE_LOG2 = 192 ** (-0.5) * LOG2E
NEG = -1e30
LANES = 128
VMEM = pl.BlockSpec(memory_space=pltpu.VMEM)
HBM = pl.BlockSpec(memory_space=pltpu.HBM)
CONTRACT_LAST = (((1,), (1,)), ((), ()))
COLUMNS = 256
QUAD = 4


def call(kernel, out_shape, in_specs, out_specs=None, scratch=(), flops=0, exps=0, nbytes=0):
    if out_specs is None:
        out_specs = jax.tree.map(lambda s: VMEM, out_shape)
    return pl.pallas_call(
        kernel,
        out_shape=out_shape,
        in_specs=in_specs,
        out_specs=out_specs,
        scratch_shapes=list(scratch),
        compiler_params=pltpu.CompilerParams(vmem_limit_bytes=40 << 20),
        cost_estimate=pl.CostEstimate(flops=flops, transcendentals=exps, bytes_accessed=nbytes),
    )


def half_at(core, half):
    return pl.ds(pl.multiple_of(core * half, LANES), half)


def head_sums(n_rows, n_heads, iq_ref, keys, w_ref, out_ref):
    rows = 256
    per = rows // n_heads
    for b in range(n_rows * n_heads // rows):
        dots = lax.dot_general(
            iq_ref[b * rows : (b + 1) * rows, :], keys, CONTRACT_LAST, preferred_element_type=F32
        )
        for i in range(per):
            row = b * per + i
            at = slice(row * n_heads, (row + 1) * n_heads)
            out_ref[row : row + 1, :] = jnp.sum(
                jnp.maximum(dots[i * n_heads : (i + 1) * n_heads, :], 0.0) * w_ref[at, 0:1],
                axis=0,
                keepdims=True,
            )


def logits_kernel(
    n_rows, n_heads, scale,
    pos_hbm, iq_hbm, ik_hbm, iw_hbm, q_hbm, lat_hbm,
    send_ref, bias_ref, iq_ref, ik_ref, w_ref, q_ref, lat_ref,
    iw_ref, pos_ref, sems,
):
    half = send_ref.shape[1]
    copies = [
        pltpu.make_async_copy(a, b, sems.at[i])
        for i, (a, b) in enumerate(
            (
                (pos_hbm, pos_ref),
                (iw_hbm, iw_ref),
                (ik_hbm, ik_ref),
                (iq_hbm, iq_ref),
                (lat_hbm, lat_ref),
                (q_hbm, q_ref),
            )
        )
    ]
    for copy in copies:
        copy.start()
    copies[0].wait()
    place = lax.axis_index("ctx") * 2 * half + lax.broadcasted_iota(jnp.int32, (8, 2 * half), 1)
    sublane = lax.broadcasted_iota(jnp.int32, (8, 1), 0)
    for first in range(0, n_rows, 8):
        pos = jnp.zeros((8, 1), jnp.int32)
        for i in range(8):
            pos = jnp.where(sublane == i, pos_ref[first + i], pos)
        bias_ref[first : first + 8, :] = jnp.where(place <= pos, 0.0, NEG)
    copies[1].wait()
    for row in range(n_rows):
        w_ref[row * n_heads : (row + 1) * n_heads, :] = jnp.broadcast_to(
            iw_ref[:, row : row + 1] * scale, (n_heads, LANES)
        )
    copies[2].wait()
    copies[3].wait()
    core = lax.axis_index("heads") & 1
    head_sums(n_rows, n_heads, iq_ref, ik_ref[half_at(1 - core, half), :], w_ref, send_ref)
    copies[4].wait()
    copies[5].wait()


def kept_logits_kernel(n_rows, n_heads, bias_ref, iq_ref, ik_ref, w_ref, keep_ref):
    half = keep_ref.shape[1]
    core = lax.axis_index("heads") & 1
    head_sums(n_rows, n_heads, iq_ref, ik_ref[half_at(core, half), :], w_ref, keep_ref)
    keep_ref[...] += bias_ref[:, half_at(core, half)]


def scores_kernel(n_rows, n_heads, bias_ref, q_ref, lat_ref, p_ref, stat_ref, s_even, s_odd):
    block = s_even.shape[0]
    keys = lat_ref.shape[1]
    steps = keys // COLUMNS
    per = block // n_heads // steps
    strips = n_rows * n_heads // block * steps
    for step in range(strips + steps):
        if step < strips:
            b, n = divmod(step, steps)
            held = s_even if b % 2 == 0 else s_odd
            held[:, n * COLUMNS : (n + 1) * COLUMNS] = jnp.dot(
                q_ref[b * block : (b + 1) * block, :],
                lat_ref[:, n * COLUMNS : (n + 1) * COLUMNS],
                preferred_element_type=F32,
            )
        if step >= steps:
            b, n = divmod(step - steps, steps)
            held = s_even if b % 2 == 0 else s_odd
            for i in range(n * per, (n + 1) * per):
                row = b * (block // n_heads) + i
                x = held[i * n_heads : (i + 1) * n_heads, :] + bias_ref[row : row + 1, :]
                top = jnp.max(x, axis=1, keepdims=True)
                e = jnp.exp2((x - top) * SCORE_LOG2)
                p_ref[row * n_heads : (row + 1) * n_heads, :] = e
                stat_ref[:, row : row + 1] = top
                stat_ref[:, n_rows + row : n_rows + row + 1] = jnp.sum(e, axis=1, keepdims=True)


def index_stats_kernel(mine_ref, other_ref, stat_ref, e_ref, out_ref, col):
    n_rows = mine_ref.shape[0]
    x = (mine_ref[...] + other_ref[...]) * LOG2E
    top = jnp.max(x, axis=1, keepdims=True)
    e = jnp.exp2(x - top)
    e_ref[...] = e
    col[:n_rows, 0:1] = top
    col[n_rows:, 0:1] = jnp.sum(e, axis=1, keepdims=True)
    n = stat_ref.shape[0]
    out_ref[:n, :] = stat_ref[...]
    out_ref[n:, :] = jnp.transpose(col[...])[: out_ref.shape[0] - n, :]


def joined(stats, unit):
    n = stats[0].shape[1] // 2
    tops = [s[:, :n] for s in stats]
    top = functools.reduce(jnp.maximum, tops)
    total = sum(s[:, n:] * jnp.exp2((t - top) * unit) for s, t in zip(stats, tops))
    return top, total


def target_sums(n_rows, n_heads, p_ref, weight, at, out_ref):
    for row in range(n_rows):
        out_ref[row : row + 1, :] = jnp.sum(
            p_ref[row * n_heads : (row + 1) * n_heads, at] * weight[:, row : row + 1],
            axis=0,
            keepdims=True,
        )


def target_kernel(n_rows, n_heads, all_ref, own_ref, p_ref, send_ref, weight_ref):
    half = send_ref.shape[1]
    n = all_ref.shape[0]
    top, total = joined([all_ref[k, :n_heads, :] for k in range(n)], SCORE_LOG2)
    weight = jnp.exp2((own_ref[:n_heads, :n_rows] - top) * SCORE_LOG2) / total
    peak, mass = joined([all_ref[k, n_heads:, :] for k in range(n)], 1.0)
    weight_ref[:n_heads, :n_rows] = weight
    for ref, first in ((weight_ref, n_heads), (send_ref, n_rows)):
        ref[first:, :n_rows] = peak
        ref[first:, n_rows : 2 * n_rows] = mass
    core = lax.axis_index("heads") & 1
    target_sums(n_rows, n_heads, p_ref, weight, half_at(1 - core, half), send_ref)


def kept_target_kernel(n_rows, n_heads, weight_ref, p_ref, keep_ref):
    core = lax.axis_index("heads") & 1
    at = half_at(core, keep_ref.shape[1])
    target_sums(n_rows, n_heads, p_ref, weight_ref[:n_heads, :n_rows], at, keep_ref)


def probs_kernel(mine_ref, other_ref, own_ref, e_ref, prob_ref, col):
    n_rows = e_ref.shape[0]
    first = mine_ref.shape[0] - 8
    peak, mass = joined([mine_ref[first:, :], other_ref[n_rows:, : 2 * n_rows]], 1.0)
    factor = jnp.exp2(own_ref[own_ref.shape[0] - 8 :, :n_rows] - peak) / mass
    col[:8, :n_rows] = factor
    prob_ref[...] = e_ref[...] * jnp.transpose(col[...])[:n_rows, 0:1]


def mask_kernel(iq_ref, ik_ref, w_ref, wm_ref, iqt_ref):
    rows = 256
    for b in range(iq_ref.shape[0] // rows):
        at = slice(b * rows, (b + 1) * rows)
        dots = lax.dot_general(iq_ref[at, :], ik_ref[...], CONTRACT_LAST, preferred_element_type=F32)
        wm_ref[at, :] = jnp.where(dots > 0.0, w_ref[at, 0:1], 0.0)
        iqt_ref[:, at] = jnp.transpose(iq_ref[at, :])


def coefficients(n_heads, g_rows, wm):
    n = g_rows.shape[1]
    g = jnp.concatenate(
        [jnp.broadcast_to(g_rows[i : i + 1, :], (n_heads, n)) for i in range(g_rows.shape[0])], axis=0
    )
    return (g * wm).astype(BF16)


def own_grads_kernel(n_heads, g_ref, wm_ref, iqt_ref, ik_ref, gq_ref, gkt_ref):
    half = g_ref.shape[1]
    at = half_at(lax.axis_index("heads") & 1, half)
    rows = 256
    per = rows // n_heads
    for b in range(wm_ref.shape[0] // rows):
        row = slice(b * rows, (b + 1) * rows)
        coef = coefficients(n_heads, g_ref[b * per : (b + 1) * per, :], wm_ref[row, at])
        gq_ref[row, :] = jnp.dot(coef, ik_ref[at, :], preferred_element_type=F32)
        term = jnp.dot(iqt_ref[:, row], coef, preferred_element_type=F32)
        if b == 0:
            gkt_ref[...] = term
        else:
            gkt_ref[...] += term


def other_grads_kernel(n_heads, k, g_ref, wm_ref, iqt_ref, ik_ref, gq_ref, *rest):
    *acc_ref, out_ref, gkt_ref = rest
    half = g_ref.shape[1]
    at = half_at(1 - (lax.axis_index("heads") & 1), half)
    rows = out_ref.shape[0]
    per = rows // n_heads
    block = (lax.axis_index("ctx") & (QUAD - 1)) ^ k
    row = pl.ds(pl.multiple_of(block * rows, rows), rows)
    coef = coefficients(
        n_heads, g_ref[pl.ds(pl.multiple_of(block * per, per), per), :], wm_ref[row, at]
    )
    out_ref[...] = gq_ref[row, :] + jnp.dot(coef, ik_ref[at, :], preferred_element_type=F32)
    term = jnp.dot(iqt_ref[:, row], coef, preferred_element_type=F32)
    gkt_ref[...] = acc_ref[0][...] + term if acc_ref else term


def key_grads_kernel(mine_ref, other_ref, *rest):
    *gk_refs, gk_t = rest
    half = mine_ref.shape[1]
    me = lax.axis_index("heads")
    gk_t[:, half_at(me & 1, half)] = mine_ref[...]
    gk_t[:, half_at(1 - (me & 1), half)] = other_ref[...]
    size = gk_refs[0].shape[0]
    for k, ref in enumerate(gk_refs):
        at = pl.multiple_of((me ^ k) * size, LANES)
        ref[...] = jnp.transpose(gk_t[:, pl.ds(at, size)])


def outputs_kernel(n_quad, *refs):
    *in_refs, gq_hbm, gk_hbm, total, sems = refs
    blocks, parts = in_refs[:n_quad], in_refs[n_quad:]
    size = blocks[0].shape[0]
    slot = lax.axis_index("ctx") & (n_quad - 1)
    copies = [
        pltpu.make_async_copy(
            ref, gq_hbm.at[pl.ds(pl.multiple_of((slot ^ k) * size, size), size), :], sems.at[k]
        )
        for k, ref in enumerate(blocks)
    ]
    for copy in copies:
        copy.start()
    total[...] = sum(ref[...] for ref in parts)
    last = pltpu.make_async_copy(total, gk_hbm, sems.at[n_quad])
    last.start()
    for copy in copies + [last]:
        copy.wait()


def body(queries, latents, index_queries, index_keys, index_weights, positions):
    n_rows, heads_local, width = queries.shape
    keys = latents.shape[0]
    index_local, depth = index_queries.shape[1:]
    n_ctx = lax.axis_size("ctx")
    n_heads = lax.axis_size("heads")
    half = keys // 2
    loss_scale = float(n_ctx * keys // 64)
    shape = jax.ShapeDtypeStruct

    def swapped(value, axis, k):
        n = lax.axis_size(axis)
        return lax.ppermute(value, axis, [(i, i ^ k) for i in range(n)])

    flat = (n_rows * index_local, depth)
    send, bias, iq, ik, w, q, lat = call(
        functools.partial(
            logits_kernel, n_rows, index_local, (index_local * n_heads * depth) ** (-0.5)
        ),
        (
            shape((n_rows, half), F32),
            shape((n_rows, keys), F32),
            shape(flat, BF16),
            shape((keys, depth), BF16),
            shape((flat[0], LANES), F32),
            shape((n_rows * heads_local, width), BF16),
            shape((width, keys), BF16),
        ),
        [HBM] * 6,
        scratch=[
            pltpu.VMEM((index_local, n_rows), F32),
            pltpu.SMEM((n_rows,), jnp.int32),
            pltpu.SemaphoreType.DMA((6,)),
        ],
        flops=flat[0] * depth * keys,
        nbytes=queries.size * 2 + latents.size * 2,
    )(
        *(
            pltpu.with_memory_space_constraint(x, pltpu.HBM)
            for x in (
                positions,
                index_queries.reshape(flat),
                index_keys,
                index_weights.T,
                queries.reshape(n_rows * heads_local, width),
                latents.T,
            )
        ),
    )
    got = swapped(send, "heads", 1)
    keep = call(
        functools.partial(kept_logits_kernel, n_rows, index_local),
        shape((n_rows, half), F32),
        [VMEM] * 4,
        flops=flat[0] * depth * keys,
    )(bias, iq, ik, w)
    logit_mine = keep + got
    logit_other = swapped(logit_mine, "heads", 2)
    probs, stats = call(
        functools.partial(scores_kernel, n_rows, heads_local),
        (shape((n_rows * heads_local, keys), F32), shape((heads_local, 2 * n_rows), F32)),
        [VMEM] * 3,
        scratch=[pltpu.VMEM((256, keys), F32)] * 2,
        flops=2 * queries.size * keys,
        exps=n_rows * heads_local * keys,
        nbytes=queries.size * 2,
    )(bias, q, lat)
    exps, stats = call(
        index_stats_kernel,
        (shape((n_rows, half), F32), shape((heads_local + 8, 2 * n_rows), F32)),
        [VMEM] * 3,
        scratch=[pltpu.VMEM((LANES, LANES), F32)],
    )(logit_mine, logit_other, stats)
    everyone = lax.all_to_all(jnp.broadcast_to(stats, (n_ctx,) + stats.shape), "ctx", 0, 0)
    send, weight = call(
        functools.partial(target_kernel, n_rows, heads_local),
        (shape((n_rows + 8, half), F32), shape((heads_local + 8, 2 * n_rows), F32)),
        [VMEM] * 3,
        flops=n_rows * heads_local * keys,
    )(everyone, stats, probs)
    got = swapped(send, "heads", 1)
    keep = call(
        functools.partial(kept_target_kernel, n_rows, heads_local),
        shape((n_rows, half), F32),
        [VMEM] * 2,
        flops=n_rows * heads_local * keys,
    )(weight, probs)
    index_probs = call(
        probs_kernel,
        shape((n_rows, half), F32),
        [VMEM] * 4,
        scratch=[pltpu.VMEM((LANES, LANES), F32)],
    )(weight, got, stats, exps)
    target = keep + got[:n_rows]
    masked, iq_t = call(
        mask_kernel,
        (shape((flat[0], keys), F32), shape(flat[::-1], BF16)),
        [VMEM] * 3,
        flops=2 * flat[0] * depth * keys,
    )(iq, ik, w)
    rest, masked, iq_t = lax.optimization_barrier((swapped(target, "heads", 2), masked, iq_t))
    target = target + rest
    grad = loss_scale * (index_probs - target * (1.0 / (heads_local * n_heads)))
    grad_other = swapped(grad, "heads", 1)
    query_sums, key_sums = call(
        functools.partial(own_grads_kernel, index_local),
        (shape(flat, F32), shape((depth, half), F32)),
        [VMEM] * 4,
        flops=2 * flat[0] * depth * keys,
    )(grad, masked, iq_t, ik)
    query_parts = [None] * QUAD
    sums = ()
    for k in range(QUAD - 1, -1, -1):
        query_parts[k], more = call(
            functools.partial(other_grads_kernel, index_local, k),
            (shape((flat[0] // QUAD, depth), F32), shape((depth, half), F32)),
            [VMEM] * (5 + len(sums)),
            flops=2 * flat[0] * depth * keys // QUAD,
        )(grad_other, masked, iq_t, ik, query_sums, *sums)
        sums = (more,)
        if k:
            query_parts[k] = swapped(query_parts[k], "ctx", k)
    owned = keys // n_heads
    key_parts = call(
        key_grads_kernel,
        (shape((owned, depth), F32),) * n_heads,
        [VMEM] * 2,
        scratch=[pltpu.VMEM((depth, keys), F32)],
    )(key_sums, *sums)
    mine = sum(query_parts)
    key_parts = [key_parts[0]] + [swapped(key_parts[k], "heads", k) for k in range(1, n_heads)]
    k = QUAD
    while k < n_ctx:
        mine = mine + swapped(mine, "ctx", k)
        k *= 2
    blocks = [mine]
    for k in range(1, QUAD):
        blocks.append(swapped(mine, "ctx", k))
    grad_queries, grad_keys = call(
        functools.partial(outputs_kernel, QUAD),
        (shape(flat, F32), shape((owned, depth), F32)),
        [VMEM] * (QUAD + n_heads),
        out_specs=(HBM, HBM),
        scratch=[pltpu.VMEM((owned, depth), F32), pltpu.SemaphoreType.DMA((QUAD + 1,))],
    )(*blocks, *key_parts)
    return grad_queries.reshape(n_rows, index_local, depth), grad_keys


def solution(mesh):
    placed = (
        P(None, "heads", None),
        P("ctx", None),
        P(None, "heads", None),
        P("ctx", None),
        P(None, "heads"),
        P(),
    )
    return jax.shard_map(
        body,
        mesh=mesh,
        in_specs=placed,
        out_specs=(P(None, "heads", None), P(("ctx", "heads"), None)),
        check_vma=False,
    )
```

```python
import functools
import math

import jax
import jax.numpy as jnp
from jax import lax
from jax.experimental import pallas as pl
from jax.experimental.pallas import tpu as pltpu
from jax.sharding import PartitionSpec as P


F32 = jnp.float32
BF16 = jnp.bfloat16
LOG2E = math.log2(math.e)
SCORE_LOG2 = 192 ** (-0.5) * LOG2E
NEG = -1e30
LANES = 128
VMEM = pl.BlockSpec(memory_space=pltpu.VMEM)
HBM = pl.BlockSpec(memory_space=pltpu.HBM)
CONTRACT_LAST = (((1,), (1,)), ((), ()))
COLUMNS = 256
QUAD = 4


def call(kernel, out_shape, in_specs, out_specs=None, scratch=(), flops=0, exps=0, nbytes=0):
    if out_specs is None:
        out_specs = jax.tree.map(lambda s: VMEM, out_shape)
    return pl.pallas_call(
        kernel,
        out_shape=out_shape,
        in_specs=in_specs,
        out_specs=out_specs,
        scratch_shapes=list(scratch),
        compiler_params=pltpu.CompilerParams(vmem_limit_bytes=40 << 20),
        cost_estimate=pl.CostEstimate(flops=flops, transcendentals=exps, bytes_accessed=nbytes),
    )


def half_at(core, half):
    return pl.ds(pl.multiple_of(core * half, LANES), half)


def head_sums(n_rows, n_heads, iq_ref, keys, w_ref, out_ref):
    rows = 256
    per = rows // n_heads
    for b in range(n_rows * n_heads // rows):
        dots = lax.dot_general(
            iq_ref[b * rows : (b + 1) * rows, :], keys, CONTRACT_LAST, preferred_element_type=F32
        )
        for i in range(per):
            row = b * per + i
            at = slice(row * n_heads, (row + 1) * n_heads)
            out_ref[row : row + 1, :] = jnp.sum(
                jnp.maximum(dots[i * n_heads : (i + 1) * n_heads, :], 0.0) * w_ref[at, 0:1],
                axis=0,
                keepdims=True,
            )


def logits_kernel(
    n_rows, n_heads, scale,
    pos_hbm, iq_hbm, ik_hbm, iw_hbm, lat_hbm,
    send_ref, bias_ref, iq_ref, ik_ref, w_ref, lat_ref,
    iw_ref, pos_ref, sems,
):
    half = send_ref.shape[1]
    copies = [
        pltpu.make_async_copy(a, b, sems.at[i])
        for i, (a, b) in enumerate(
            (
                (pos_hbm, pos_ref),
                (iw_hbm, iw_ref),
                (ik_hbm, ik_ref),
                (iq_hbm, iq_ref),
                (lat_hbm, lat_ref),
            )
        )
    ]
    for copy in copies:
        copy.start()
    copies[0].wait()
    place = lax.axis_index("ctx") * 2 * half + lax.broadcasted_iota(jnp.int32, (8, 2 * half), 1)
    sublane = lax.broadcasted_iota(jnp.int32, (8, 1), 0)
    for first in range(0, n_rows, 8):
        pos = jnp.zeros((8, 1), jnp.int32)
        for i in range(8):
            pos = jnp.where(sublane == i, pos_ref[first + i], pos)
        bias_ref[first : first + 8, :] = jnp.where(place <= pos, 0.0, NEG)
    copies[1].wait()
    for row in range(n_rows):
        w_ref[row * n_heads : (row + 1) * n_heads, :] = jnp.broadcast_to(
            iw_ref[:, row : row + 1] * scale, (n_heads, LANES)
        )
    copies[2].wait()
    copies[3].wait()
    core = lax.axis_index("heads") & 1
    head_sums(n_rows, n_heads, iq_ref, ik_ref[half_at(1 - core, half), :], w_ref, send_ref)
    copies[4].wait()


def kept_logits_kernel(
    n_rows, n_heads, bias_ref, iq_ref, ik_ref, w_ref, q_hbm, keep_ref, q_ref, sem
):
    copy = pltpu.make_async_copy(q_hbm, q_ref, sem)
    copy.start()
    half = keep_ref.shape[1]
    core = lax.axis_index("heads") & 1
    head_sums(n_rows, n_heads, iq_ref, ik_ref[half_at(core, half), :], w_ref, keep_ref)
    keep_ref[...] += bias_ref[:, half_at(core, half)]
    copy.wait()


def scores_kernel(n_rows, n_heads, bias_ref, q_ref, lat_ref, p_ref, stat_ref, s_even, s_odd):
    block = s_even.shape[0]
    keys = lat_ref.shape[1]
    steps = keys // COLUMNS
    per = block // n_heads // steps
    strips = n_rows * n_heads // block * steps
    for step in range(strips + steps):
        if step < strips:
            b, n = divmod(step, steps)
            held = s_even if b % 2 == 0 else s_odd
            held[:, n * COLUMNS : (n + 1) * COLUMNS] = jnp.dot(
                q_ref[b * block : (b + 1) * block, :],
                lat_ref[:, n * COLUMNS : (n + 1) * COLUMNS],
                preferred_element_type=F32,
            )
        if step >= steps:
            b, n = divmod(step - steps, steps)
            held = s_even if b % 2 == 0 else s_odd
            for i in range(n * per, (n + 1) * per):
                row = b * (block // n_heads) + i
                x = held[i * n_heads : (i + 1) * n_heads, :] + bias_ref[row : row + 1, :]
                top = jnp.max(x, axis=1, keepdims=True)
                e = jnp.exp2((x - top) * SCORE_LOG2)
                p_ref[row * n_heads : (row + 1) * n_heads, :] = e
                stat_ref[:, row : row + 1] = top
                stat_ref[:, n_rows + row : n_rows + row + 1] = jnp.sum(e, axis=1, keepdims=True)


def index_stats_kernel(mine_ref, other_ref, stat_ref, e_ref, out_ref, col):
    n_rows = mine_ref.shape[0]
    x = (mine_ref[...] + other_ref[...]) * LOG2E
    top = jnp.max(x, axis=1, keepdims=True)
    e = jnp.exp2(x - top)
    e_ref[...] = e
    col[:n_rows, 0:1] = top
    col[n_rows:, 0:1] = jnp.sum(e, axis=1, keepdims=True)
    n = stat_ref.shape[0] // 2
    size = stat_ref[:, :n_rows] * SCORE_LOG2 + jnp.log2(stat_ref[:, n_rows:])
    out_ref[:n, :n_rows] = size[:n, :]
    out_ref[:n, n_rows:] = size[n:, :]
    out_ref[n:, :] = jnp.transpose(col[...])[: out_ref.shape[0] - n, :]


def joined(stats):
    n = stats[0].shape[1] // 2
    tops = [s[:, :n] for s in stats]
    top = functools.reduce(jnp.maximum, tops)
    total = sum(s[:, n:] * jnp.exp2(t - top) for s, t in zip(stats, tops))
    return top, total


def target_sums(n_rows, n_heads, p_ref, weight, at, out_ref):
    for row in range(n_rows):
        out_ref[row : row + 1, :] = jnp.sum(
            p_ref[row * n_heads : (row + 1) * n_heads, at] * weight[:, row : row + 1],
            axis=0,
            keepdims=True,
        )


def target_kernel(n_rows, n_heads, all_ref, own_ref, p_ref, send_ref, weight_ref):
    half = send_ref.shape[1]
    n = all_ref.shape[0]
    some = n_heads // 2
    sizes = [all_ref[k, :some, :] for k in range(n)]
    top = functools.reduce(jnp.maximum, sizes)
    total = sum(jnp.exp2(s - top) for s in sizes)
    tops = own_ref[:, :n_rows] * SCORE_LOG2
    weight = jnp.concatenate(
        [
            jnp.exp2(tops[:some, :] - top[:, :n_rows]) / total[:, :n_rows],
            jnp.exp2(tops[some:, :] - top[:, n_rows:]) / total[:, n_rows:],
        ],
        axis=0,
    )
    peak, mass = joined([all_ref[k, some:, :] for k in range(n)])
    weight_ref[:n_heads, :n_rows] = weight
    for ref, first in ((weight_ref, n_heads), (send_ref, n_rows)):
        ref[first:, :n_rows] = peak
        ref[first:, n_rows : 2 * n_rows] = mass
    core = lax.axis_index("heads") & 1
    target_sums(n_rows, n_heads, p_ref, weight, half_at(1 - core, half), send_ref)


def kept_target_kernel(n_rows, n_heads, weight_ref, p_ref, keep_ref):
    core = lax.axis_index("heads") & 1
    at = half_at(core, keep_ref.shape[1])
    target_sums(n_rows, n_heads, p_ref, weight_ref[:n_heads, :n_rows], at, keep_ref)


def probs_kernel(mine_ref, other_ref, own_ref, e_ref, prob_ref, col):
    n_rows = e_ref.shape[0]
    first = mine_ref.shape[0] - 8
    peak, mass = joined([mine_ref[first:, :], other_ref[n_rows:, : 2 * n_rows]])
    factor = jnp.exp2(own_ref[own_ref.shape[0] - 8 :, :n_rows] - peak) / mass
    col[:8, :n_rows] = factor
    prob_ref[...] = e_ref[...] * jnp.transpose(col[...])[:n_rows, 0:1]


def mask_kernel(iq_ref, ik_ref, w_ref, wm_ref, iqt_ref):
    rows = 256
    for b in range(iq_ref.shape[0] // rows):
        at = slice(b * rows, (b + 1) * rows)
        dots = lax.dot_general(iq_ref[at, :], ik_ref[...], CONTRACT_LAST, preferred_element_type=F32)
        wm_ref[at, :] = jnp.where(dots > 0.0, w_ref[at, 0:1], 0.0)
        iqt_ref[:, at] = jnp.transpose(iq_ref[at, :])


def coefficients(n_heads, g_rows, wm):
    n = g_rows.shape[1]
    g = jnp.concatenate(
        [jnp.broadcast_to(g_rows[i : i + 1, :], (n_heads, n)) for i in range(g_rows.shape[0])], axis=0
    )
    return (g * wm).astype(BF16)


def own_grads_kernel(n_heads, g_ref, wm_ref, iqt_ref, ik_ref, gq_ref, gkt_ref):
    half = g_ref.shape[1]
    at = half_at(lax.axis_index("heads") & 1, half)
    rows = 256
    per = rows // n_heads
    for b in range(wm_ref.shape[0] // rows):
        row = slice(b * rows, (b + 1) * rows)
        coef = coefficients(n_heads, g_ref[b * per : (b + 1) * per, :], wm_ref[row, at])
        gq_ref[row, :] = jnp.dot(coef, ik_ref[at, :], preferred_element_type=F32)
        term = jnp.dot(iqt_ref[:, row], coef, preferred_element_type=F32)
        if b == 0:
            gkt_ref[...] = term
        else:
            gkt_ref[...] += term


def other_grads_kernel(n_heads, k, g_ref, wm_ref, iqt_ref, ik_ref, gq_ref, *rest):
    *acc_ref, out_ref, gkt_ref = rest
    half = g_ref.shape[1]
    at = half_at(1 - (lax.axis_index("heads") & 1), half)
    rows = out_ref.shape[0]
    per = rows // n_heads
    block = (lax.axis_index("ctx") & (QUAD - 1)) ^ k
    row = pl.ds(pl.multiple_of(block * rows, rows), rows)
    coef = coefficients(
        n_heads, g_ref[pl.ds(pl.multiple_of(block * per, per), per), :], wm_ref[row, at]
    )
    out_ref[...] = gq_ref[row, :] + jnp.dot(coef, ik_ref[at, :], preferred_element_type=F32)
    term = jnp.dot(iqt_ref[:, row], coef, preferred_element_type=F32)
    gkt_ref[...] = acc_ref[0][...] + term if acc_ref else term


def key_grads_kernel(mine_ref, other_ref, *rest):
    *gk_refs, gk_t = rest
    half = mine_ref.shape[1]
    me = lax.axis_index("heads")
    gk_t[:, half_at(me & 1, half)] = mine_ref[...]
    gk_t[:, half_at(1 - (me & 1), half)] = other_ref[...]
    size = gk_refs[0].shape[0]
    for k, ref in enumerate(gk_refs):
        at = pl.multiple_of((me ^ k) * size, LANES)
        ref[...] = jnp.transpose(gk_t[:, pl.ds(at, size)])


def outputs_kernel(n_quad, *refs):
    *in_refs, gq_hbm, gk_hbm, total, sems = refs
    blocks, parts = in_refs[:n_quad], in_refs[n_quad:]
    size = blocks[0].shape[0]
    slot = lax.axis_index("ctx") & (n_quad - 1)
    copies = [
        pltpu.make_async_copy(
            ref, gq_hbm.at[pl.ds(pl.multiple_of((slot ^ k) * size, size), size), :], sems.at[k]
        )
        for k, ref in enumerate(blocks)
    ]
    for copy in copies:
        copy.start()
    total[...] = sum(ref[...] for ref in parts)
    last = pltpu.make_async_copy(total, gk_hbm, sems.at[n_quad])
    last.start()
    for copy in copies + [last]:
        copy.wait()


def body(queries, latents, index_queries, index_keys, index_weights, positions):
    n_rows, heads_local, width = queries.shape
    keys = latents.shape[0]
    index_local, depth = index_queries.shape[1:]
    n_ctx = lax.axis_size("ctx")
    n_heads = lax.axis_size("heads")
    half = keys // 2
    loss_scale = float(n_ctx * keys // 64)
    shape = jax.ShapeDtypeStruct

    def swapped(value, axis, k):
        n = lax.axis_size(axis)
        return lax.ppermute(value, axis, [(i, i ^ k) for i in range(n)])

    flat = (n_rows * index_local, depth)
    send, bias, iq, ik, w, lat = call(
        functools.partial(
            logits_kernel, n_rows, index_local, (index_local * n_heads * depth) ** (-0.5)
        ),
        (
            shape((n_rows, half), F32),
            shape((n_rows, keys), F32),
            shape(flat, BF16),
            shape((keys, depth), BF16),
            shape((flat[0], LANES), F32),
            shape((width, keys), BF16),
        ),
        [HBM] * 5,
        scratch=[
            pltpu.VMEM((index_local, n_rows), F32),
            pltpu.SMEM((n_rows,), jnp.int32),
            pltpu.SemaphoreType.DMA((5,)),
        ],
        flops=flat[0] * depth * keys,
        nbytes=latents.size * 2,
    )(
        *(
            pltpu.with_memory_space_constraint(x, pltpu.HBM)
            for x in (
                positions,
                index_queries.reshape(flat),
                index_keys,
                index_weights.T,
                latents.T,
            )
        )
    )
    got = swapped(send, "heads", 1)
    flat_queries = pltpu.with_memory_space_constraint(
        queries.reshape(n_rows * heads_local, width), pltpu.HBM
    )
    keep, q = call(
        functools.partial(kept_logits_kernel, n_rows, index_local),
        (shape((n_rows, half), F32), shape(flat_queries.shape, BF16)),
        [VMEM] * 4 + [HBM],
        scratch=[pltpu.SemaphoreType.DMA],
        flops=flat[0] * depth * keys,
        nbytes=queries.size * 2,
    )(bias, iq, ik, w, flat_queries)
    logit_mine = keep + got
    logit_other = swapped(logit_mine, "heads", 2)
    probs, stats = call(
        functools.partial(scores_kernel, n_rows, heads_local),
        (shape((n_rows * heads_local, keys), F32), shape((heads_local, 2 * n_rows), F32)),
        [VMEM] * 3,
        scratch=[pltpu.VMEM((256, keys), F32)] * 2,
        flops=2 * queries.size * keys,
        exps=n_rows * heads_local * keys,
        nbytes=queries.size * 2,
    )(bias, q, lat)
    exps, sizes = call(
        index_stats_kernel,
        (shape((n_rows, half), F32), shape((heads_local // 2 + 8, 2 * n_rows), F32)),
        [VMEM] * 3,
        scratch=[pltpu.VMEM((LANES, LANES), F32)],
    )(logit_mine, logit_other, stats)
    everyone = lax.all_to_all(jnp.broadcast_to(sizes, (n_ctx,) + sizes.shape), "ctx", 0, 0)
    send, weight = call(
        functools.partial(target_kernel, n_rows, heads_local),
        (shape((n_rows + 8, half), F32), shape((heads_local + 8, 2 * n_rows), F32)),
        [VMEM] * 3,
        flops=n_rows * heads_local * keys,
    )(everyone, stats, probs)
    got = swapped(send, "heads", 1)
    keep = call(
        functools.partial(kept_target_kernel, n_rows, heads_local),
        shape((n_rows, half), F32),
        [VMEM] * 2,
        flops=n_rows * heads_local * keys,
    )(weight, probs)
    index_probs = call(
        probs_kernel,
        shape((n_rows, half), F32),
        [VMEM] * 4,
        scratch=[pltpu.VMEM((LANES, LANES), F32)],
    )(weight, got, sizes, exps)
    target = keep + got[:n_rows]
    masked, iq_t = call(
        mask_kernel,
        (shape((flat[0], keys), F32), shape(flat[::-1], BF16)),
        [VMEM] * 3,
        flops=2 * flat[0] * depth * keys,
    )(iq, ik, w)
    rest, masked, iq_t = lax.optimization_barrier((swapped(target, "heads", 2), masked, iq_t))
    target = target + rest
    grad = loss_scale * (index_probs - target * (1.0 / (heads_local * n_heads)))
    grad_other = swapped(grad, "heads", 1)
    query_sums, key_sums = call(
        functools.partial(own_grads_kernel, index_local),
        (shape(flat, F32), shape((depth, half), F32)),
        [VMEM] * 4,
        flops=2 * flat[0] * depth * keys,
    )(grad, masked, iq_t, ik)
    query_parts = [None] * QUAD
    sums = ()
    for k in range(QUAD - 1, -1, -1):
        query_parts[k], more = call(
            functools.partial(other_grads_kernel, index_local, k),
            (shape((flat[0] // QUAD, depth), F32), shape((depth, half), F32)),
            [VMEM] * (5 + len(sums)),
            flops=2 * flat[0] * depth * keys // QUAD,
        )(grad_other, masked, iq_t, ik, query_sums, *sums)
        sums = (more,)
        if k:
            query_parts[k] = swapped(query_parts[k], "ctx", k)
    owned = keys // n_heads
    key_parts = call(
        key_grads_kernel,
        (shape((owned, depth), F32),) * n_heads,
        [VMEM] * 2,
        scratch=[pltpu.VMEM((depth, keys), F32)],
    )(key_sums, *sums)
    mine = sum(query_parts)
    key_parts = [key_parts[0]] + [swapped(key_parts[k], "heads", k) for k in range(1, n_heads)]
    k = QUAD
    while k < n_ctx:
        mine = mine + swapped(mine, "ctx", k)
        k *= 2
    blocks = [mine]
    for k in range(1, QUAD):
        blocks.append(swapped(mine, "ctx", k))
    grad_queries, grad_keys = call(
        functools.partial(outputs_kernel, QUAD),
        (shape(flat, F32), shape((owned, depth), F32)),
        [VMEM] * (QUAD + n_heads),
        out_specs=(HBM, HBM),
        scratch=[pltpu.VMEM((owned, depth), F32), pltpu.SemaphoreType.DMA((QUAD + 1,))],
    )(*blocks, *key_parts)
    return grad_queries.reshape(n_rows, index_local, depth), grad_keys


def solution(mesh):
    placed = (
        P(None, "heads", None),
        P("ctx", None),
        P(None, "heads", None),
        P("ctx", None),
        P(None, "heads"),
        P(),
    )
    return jax.shard_map(
        body,
        mesh=mesh,
        in_specs=placed,
        out_specs=(P(None, "heads", None), P(("ctx", "heads"), None)),
        check_vma=False,
    )
```

```python
import functools
import math

import jax
import jax.numpy as jnp
from jax import lax
from jax.experimental import pallas as pl
from jax.experimental.pallas import tpu as pltpu
from jax.sharding import PartitionSpec as P


F32 = jnp.float32
BF16 = jnp.bfloat16
LOG2E = math.log2(math.e)
SCORE_LOG2 = 192 ** (-0.5) * LOG2E
NEG = -1e30
LANES = 128
VMEM = pl.BlockSpec(memory_space=pltpu.VMEM)
HBM = pl.BlockSpec(memory_space=pltpu.HBM)
CONTRACT_LAST = (((1,), (1,)), ((), ()))
QUAD = 4


def call(kernel, out_shape, in_specs, out_specs=None, scratch=(), flops=0, exps=0, nbytes=0):
    if out_specs is None:
        out_specs = jax.tree.map(lambda s: VMEM, out_shape)
    return pl.pallas_call(
        kernel,
        out_shape=out_shape,
        in_specs=in_specs,
        out_specs=out_specs,
        scratch_shapes=list(scratch),
        compiler_params=pltpu.CompilerParams(vmem_limit_bytes=40 << 20),
        cost_estimate=pl.CostEstimate(flops=flops, transcendentals=exps, bytes_accessed=nbytes),
    )


def half_at(core, half):
    return pl.ds(pl.multiple_of(core * half, LANES), half)


def head_sums(n_rows, n_heads, iq_ref, keys, w_ref, out_ref):
    rows = 256
    per = rows // n_heads
    for b in range(n_rows * n_heads // rows):
        dots = lax.dot_general(
            iq_ref[b * rows : (b + 1) * rows, :], keys, CONTRACT_LAST, preferred_element_type=F32
        )
        for i in range(per):
            row = b * per + i
            at = slice(row * n_heads, (row + 1) * n_heads)
            out_ref[row : row + 1, :] = jnp.sum(
                jnp.maximum(dots[i * n_heads : (i + 1) * n_heads, :], 0.0) * w_ref[at, 0:1],
                axis=0,
                keepdims=True,
            )


def logits_kernel(
    n_rows, n_heads, scale,
    pos_hbm, iq_hbm, ik_hbm, iw_hbm, lat_hbm,
    send_ref, bias_ref, iq_ref, ik_ref, w_ref, lat_ref,
    iw_ref, pos_ref, sems,
):
    half = send_ref.shape[1]
    copies = [
        pltpu.make_async_copy(a, b, sems.at[i])
        for i, (a, b) in enumerate(
            (
                (pos_hbm, pos_ref),
                (iw_hbm, iw_ref),
                (ik_hbm, ik_ref),
                (iq_hbm, iq_ref),
                (lat_hbm, lat_ref),
            )
        )
    ]
    for copy in copies:
        copy.start()
    copies[0].wait()
    place = lax.axis_index("ctx") * 2 * half + lax.broadcasted_iota(jnp.int32, (8, 2 * half), 1)
    sublane = lax.broadcasted_iota(jnp.int32, (8, 1), 0)
    for first in range(0, n_rows, 8):
        pos = jnp.zeros((8, 1), jnp.int32)
        for i in range(8):
            pos = jnp.where(sublane == i, pos_ref[first + i], pos)
        bias_ref[first : first + 8, :] = jnp.where(place <= pos, 0.0, NEG)
    copies[1].wait()
    for row in range(n_rows):
        w_ref[row * n_heads : (row + 1) * n_heads, :] = jnp.broadcast_to(
            iw_ref[:, row : row + 1] * scale, (n_heads, LANES)
        )
    copies[2].wait()
    copies[3].wait()
    core = lax.axis_index("heads") & 1
    head_sums(n_rows, n_heads, iq_ref, ik_ref[half_at(1 - core, half), :], w_ref, send_ref)
    copies[4].wait()


def kept_logits_kernel(
    n_rows, n_heads, bias_ref, iq_ref, ik_ref, w_ref, q_hbm, keep_ref, q_ref, sem
):
    copy = pltpu.make_async_copy(q_hbm.at[pl.ds(0, q_ref.shape[0]), :], q_ref, sem)
    copy.start()
    half = keep_ref.shape[1]
    core = lax.axis_index("heads") & 1
    head_sums(n_rows, n_heads, iq_ref, ik_ref[half_at(core, half), :], w_ref, keep_ref)
    keep_ref[...] += bias_ref[:, half_at(core, half)]
    copy.wait()


def scores_kernel(
    n_rows, n_heads, bias_ref, q_ref, q_hbm, lat_ref, p_ref, stat_ref, s_even, s_odd, q_rest, sem
):
    ready = q_ref.shape[0]
    copy = pltpu.make_async_copy(q_hbm.at[pl.ds(ready, q_rest.shape[0]), :], q_rest, sem)
    copy.start()
    block = s_even.shape[0]
    blocks = n_rows * n_heads // block

    def dots(b):
        held = s_even if b % 2 == 0 else s_odd
        first = b * block
        if first == ready:
            copy.wait()
        source = q_ref[first : first + block, :] if first < ready else q_rest[
            first - ready : first - ready + block, :
        ]
        held[...] = jnp.dot(source, lat_ref[...], preferred_element_type=F32)

    dots(0)
    for b in range(blocks):
        if b + 1 < blocks:
            dots(b + 1)
        held = s_even if b % 2 == 0 else s_odd
        for i in range(block // n_heads):
            row = b * (block // n_heads) + i
            x = held[i * n_heads : (i + 1) * n_heads, :] + bias_ref[row : row + 1, :]
            top = jnp.max(x, axis=1, keepdims=True)
            e = jnp.exp2((x - top) * SCORE_LOG2)
            p_ref[row * n_heads : (row + 1) * n_heads, :] = e
            stat_ref[:, row : row + 1] = top
            stat_ref[:, n_rows + row : n_rows + row + 1] = jnp.sum(e, axis=1, keepdims=True)


def index_stats_kernel(mine_ref, other_ref, stat_ref, e_ref, out_ref, col):
    n_rows = mine_ref.shape[0]
    x = (mine_ref[...] + other_ref[...]) * LOG2E
    top = jnp.max(x, axis=1, keepdims=True)
    e = jnp.exp2(x - top)
    e_ref[...] = e
    col[:n_rows, 0:1] = top
    col[n_rows:, 0:1] = jnp.sum(e, axis=1, keepdims=True)
    n = stat_ref.shape[0] // 2
    size = stat_ref[:, :n_rows] * SCORE_LOG2 + jnp.log2(stat_ref[:, n_rows:])
    out_ref[:n, :n_rows] = size[:n, :]
    out_ref[:n, n_rows:] = size[n:, :]
    out_ref[n:, :] = jnp.transpose(col[...])[: out_ref.shape[0] - n, :]


def joined(stats):
    n = stats[0].shape[1] // 2
    tops = [s[:, :n] for s in stats]
    top = functools.reduce(jnp.maximum, tops)
    total = sum(s[:, n:] * jnp.exp2(t - top) for s, t in zip(stats, tops))
    return top, total


def target_sums(n_rows, n_heads, p_ref, weight, at, out_ref):
    for row in range(n_rows):
        out_ref[row : row + 1, :] = jnp.sum(
            p_ref[row * n_heads : (row + 1) * n_heads, at] * weight[:, row : row + 1],
            axis=0,
            keepdims=True,
        )


def target_kernel(n_rows, n_heads, all_ref, own_ref, p_ref, send_ref, weight_ref):
    half = send_ref.shape[1]
    n = all_ref.shape[0]
    some = n_heads // 2
    sizes = [all_ref[k, :some, :] for k in range(n)]
    top = functools.reduce(jnp.maximum, sizes)
    total = sum(jnp.exp2(s - top) for s in sizes)
    tops = own_ref[:, :n_rows] * SCORE_LOG2
    weight = jnp.concatenate(
        [
            jnp.exp2(tops[:some, :] - top[:, :n_rows]) / total[:, :n_rows],
            jnp.exp2(tops[some:, :] - top[:, n_rows:]) / total[:, n_rows:],
        ],
        axis=0,
    )
    peak, mass = joined([all_ref[k, some:, :] for k in range(n)])
    weight_ref[:n_heads, :n_rows] = weight
    for ref, first in ((weight_ref, n_heads), (send_ref, n_rows)):
        ref[first:, :n_rows] = peak
        ref[first:, n_rows : 2 * n_rows] = mass
    core = lax.axis_index("heads") & 1
    target_sums(n_rows, n_heads, p_ref, weight, half_at(1 - core, half), send_ref)


def kept_target_kernel(n_rows, n_heads, weight_ref, p_ref, keep_ref):
    core = lax.axis_index("heads") & 1
    at = half_at(core, keep_ref.shape[1])
    target_sums(n_rows, n_heads, p_ref, weight_ref[:n_heads, :n_rows], at, keep_ref)


def probs_kernel(mine_ref, other_ref, own_ref, e_ref, prob_ref, col):
    n_rows = e_ref.shape[0]
    first = mine_ref.shape[0] - 8
    peak, mass = joined([mine_ref[first:, :], other_ref[n_rows:, : 2 * n_rows]])
    factor = jnp.exp2(own_ref[own_ref.shape[0] - 8 :, :n_rows] - peak) / mass
    col[:8, :n_rows] = factor
    prob_ref[...] = e_ref[...] * jnp.transpose(col[...])[:n_rows, 0:1]


def mask_kernel(iq_ref, ik_ref, w_ref, wm_ref, iqt_ref):
    rows = 256
    for b in range(iq_ref.shape[0] // rows):
        at = slice(b * rows, (b + 1) * rows)
        dots = lax.dot_general(iq_ref[at, :], ik_ref[...], CONTRACT_LAST, preferred_element_type=F32)
        wm_ref[at, :] = jnp.where(dots > 0.0, w_ref[at, 0:1], 0.0)
        iqt_ref[:, at] = jnp.transpose(iq_ref[at, :])


def coefficients(n_heads, g_rows, wm):
    n = g_rows.shape[1]
    g = jnp.concatenate(
        [jnp.broadcast_to(g_rows[i : i + 1, :], (n_heads, n)) for i in range(g_rows.shape[0])], axis=0
    )
    return (g * wm).astype(BF16)


def own_grads_kernel(n_heads, g_ref, wm_ref, iqt_ref, ik_ref, gq_ref, gkt_ref):
    half = g_ref.shape[1]
    at = half_at(lax.axis_index("heads") & 1, half)
    rows = 256
    per = rows // n_heads
    for b in range(wm_ref.shape[0] // rows):
        row = slice(b * rows, (b + 1) * rows)
        coef = coefficients(n_heads, g_ref[b * per : (b + 1) * per, :], wm_ref[row, at])
        gq_ref[row, :] = jnp.dot(coef, ik_ref[at, :], preferred_element_type=F32)
        term = jnp.dot(iqt_ref[:, row], coef, preferred_element_type=F32)
        if b == 0:
            gkt_ref[...] = term
        else:
            gkt_ref[...] += term


def other_grads_kernel(n_heads, k, g_ref, wm_ref, iqt_ref, ik_ref, gq_ref, *rest):
    *acc_ref, out_ref, gkt_ref = rest
    half = g_ref.shape[1]
    at = half_at(1 - (lax.axis_index("heads") & 1), half)
    rows = out_ref.shape[0]
    per = rows // n_heads
    block = (lax.axis_index("ctx") & (QUAD - 1)) ^ k
    row = pl.ds(pl.multiple_of(block * rows, rows), rows)
    coef = coefficients(
        n_heads, g_ref[pl.ds(pl.multiple_of(block * per, per), per), :], wm_ref[row, at]
    )
    out_ref[...] = gq_ref[row, :] + jnp.dot(coef, ik_ref[at, :], preferred_element_type=F32)
    term = jnp.dot(iqt_ref[:, row], coef, preferred_element_type=F32)
    gkt_ref[...] = acc_ref[0][...] + term if acc_ref else term


def key_grads_kernel(mine_ref, other_ref, *rest):
    *gk_refs, gk_t = rest
    half = mine_ref.shape[1]
    me = lax.axis_index("heads")
    gk_t[:, half_at(me & 1, half)] = mine_ref[...]
    gk_t[:, half_at(1 - (me & 1), half)] = other_ref[...]
    size = gk_refs[0].shape[0]
    for k, ref in enumerate(gk_refs):
        at = pl.multiple_of((me ^ k) * size, LANES)
        ref[...] = jnp.transpose(gk_t[:, pl.ds(at, size)])


def outputs_kernel(n_quad, *refs):
    *in_refs, gq_hbm, gk_hbm, total, sems = refs
    blocks, parts = in_refs[:n_quad], in_refs[n_quad:]
    size = blocks[0].shape[0]
    slot = lax.axis_index("ctx") & (n_quad - 1)
    copies = [
        pltpu.make_async_copy(
            ref, gq_hbm.at[pl.ds(pl.multiple_of((slot ^ k) * size, size), size), :], sems.at[k]
        )
        for k, ref in enumerate(blocks)
    ]
    for copy in copies:
        copy.start()
    total[...] = sum(ref[...] for ref in parts)
    last = pltpu.make_async_copy(total, gk_hbm, sems.at[n_quad])
    last.start()
    for copy in copies + [last]:
        copy.wait()


def body(queries, latents, index_queries, index_keys, index_weights, positions):
    n_rows, heads_local, width = queries.shape
    keys = latents.shape[0]
    index_local, depth = index_queries.shape[1:]
    n_ctx = lax.axis_size("ctx")
    n_heads = lax.axis_size("heads")
    half = keys // 2
    loss_scale = float(n_ctx * keys // 64)
    shape = jax.ShapeDtypeStruct

    def swapped(value, axis, k):
        n = lax.axis_size(axis)
        return lax.ppermute(value, axis, [(i, i ^ k) for i in range(n)])

    flat = (n_rows * index_local, depth)
    send, bias, iq, ik, w, lat = call(
        functools.partial(
            logits_kernel, n_rows, index_local, (index_local * n_heads * depth) ** (-0.5)
        ),
        (
            shape((n_rows, half), F32),
            shape((n_rows, keys), F32),
            shape(flat, BF16),
            shape((keys, depth), BF16),
            shape((flat[0], LANES), F32),
            shape((width, keys), BF16),
        ),
        [HBM] * 5,
        scratch=[
            pltpu.VMEM((index_local, n_rows), F32),
            pltpu.SMEM((n_rows,), jnp.int32),
            pltpu.SemaphoreType.DMA((5,)),
        ],
        flops=flat[0] * depth * keys,
        nbytes=latents.size * 2,
    )(
        *(
            pltpu.with_memory_space_constraint(x, pltpu.HBM)
            for x in (
                positions,
                index_queries.reshape(flat),
                index_keys,
                index_weights.T,
                latents.T,
            )
        )
    )
    got = swapped(send, "heads", 1)
    flat_queries = pltpu.with_memory_space_constraint(
        queries.reshape(n_rows * heads_local, width), pltpu.HBM
    )
    ready = n_rows * heads_local // 2
    keep, q = call(
        functools.partial(kept_logits_kernel, n_rows, index_local),
        (shape((n_rows, half), F32), shape((ready, width), BF16)),
        [VMEM] * 4 + [HBM],
        scratch=[pltpu.SemaphoreType.DMA],
        flops=flat[0] * depth * keys,
        nbytes=queries.size * 2,
    )(bias, iq, ik, w, flat_queries)
    logit_mine = keep + got
    logit_other = swapped(logit_mine, "heads", 2)
    probs, stats = call(
        functools.partial(scores_kernel, n_rows, heads_local),
        (shape((n_rows * heads_local, keys), F32), shape((heads_local, 2 * n_rows), F32)),
        [VMEM, VMEM, HBM, VMEM],
        scratch=[pltpu.VMEM((256, keys), F32)] * 2
        + [pltpu.VMEM((n_rows * heads_local - ready, width), BF16), pltpu.SemaphoreType.DMA],
        flops=2 * queries.size * keys,
        exps=n_rows * heads_local * keys,
        nbytes=queries.size * 2,
    )(bias, q, flat_queries, lat)
    exps, sizes = call(
        index_stats_kernel,
        (shape((n_rows, half), F32), shape((heads_local // 2 + 8, 2 * n_rows), F32)),
        [VMEM] * 3,
        scratch=[pltpu.VMEM((LANES, LANES), F32)],
    )(logit_mine, logit_other, stats)
    everyone = lax.all_to_all(jnp.broadcast_to(sizes, (n_ctx,) + sizes.shape), "ctx", 0, 0)
    send, weight = call(
        functools.partial(target_kernel, n_rows, heads_local),
        (shape((n_rows + 8, half), F32), shape((heads_local + 8, 2 * n_rows), F32)),
        [VMEM] * 3,
        flops=n_rows * heads_local * keys,
    )(everyone, stats, probs)
    got = swapped(send, "heads", 1)
    keep = call(
        functools.partial(kept_target_kernel, n_rows, heads_local),
        shape((n_rows, half), F32),
        [VMEM] * 2,
        flops=n_rows * heads_local * keys,
    )(weight, probs)
    index_probs = call(
        probs_kernel,
        shape((n_rows, half), F32),
        [VMEM] * 4,
        scratch=[pltpu.VMEM((LANES, LANES), F32)],
    )(weight, got, sizes, exps)
    target = keep + got[:n_rows]
    masked, iq_t = call(
        mask_kernel,
        (shape((flat[0], keys), F32), shape(flat[::-1], BF16)),
        [VMEM] * 3,
        flops=2 * flat[0] * depth * keys,
    )(iq, ik, w)
    rest, masked, iq_t = lax.optimization_barrier((swapped(target, "heads", 2), masked, iq_t))
    target = target + rest
    grad = loss_scale * (index_probs - target * (1.0 / (heads_local * n_heads)))
    grad_other = swapped(grad, "heads", 1)
    query_sums, key_sums = call(
        functools.partial(own_grads_kernel, index_local),
        (shape(flat, F32), shape((depth, half), F32)),
        [VMEM] * 4,
        flops=2 * flat[0] * depth * keys,
    )(grad, masked, iq_t, ik)
    query_parts = [None] * QUAD
    sums = ()
    for k in range(QUAD - 1, -1, -1):
        query_parts[k], more = call(
            functools.partial(other_grads_kernel, index_local, k),
            (shape((flat[0] // QUAD, depth), F32), shape((depth, half), F32)),
            [VMEM] * (5 + len(sums)),
            flops=2 * flat[0] * depth * keys // QUAD,
        )(grad_other, masked, iq_t, ik, query_sums, *sums)
        sums = (more,)
        if k:
            query_parts[k] = swapped(query_parts[k], "ctx", k)
    owned = keys // n_heads
    key_parts = call(
        key_grads_kernel,
        (shape((owned, depth), F32),) * n_heads,
        [VMEM] * 2,
        scratch=[pltpu.VMEM((depth, keys), F32)],
    )(key_sums, *sums)
    mine = sum(query_parts)
    key_parts = [key_parts[0]] + [swapped(key_parts[k], "heads", k) for k in range(1, n_heads)]
    k = QUAD
    while k < n_ctx:
        mine = mine + swapped(mine, "ctx", k)
        k *= 2
    blocks = [mine]
    for k in range(1, QUAD):
        blocks.append(swapped(mine, "ctx", k))
    grad_queries, grad_keys = call(
        functools.partial(outputs_kernel, QUAD),
        (shape(flat, F32), shape((owned, depth), F32)),
        [VMEM] * (QUAD + n_heads),
        out_specs=(HBM, HBM),
        scratch=[pltpu.VMEM((owned, depth), F32), pltpu.SemaphoreType.DMA((QUAD + 1,))],
    )(*blocks, *key_parts)
    return grad_queries.reshape(n_rows, index_local, depth), grad_keys


def solution(mesh):
    placed = (
        P(None, "heads", None),
        P("ctx", None),
        P(None, "heads", None),
        P("ctx", None),
        P(None, "heads"),
        P(),
    )
    return jax.shard_map(
        body,
        mesh=mesh,
        in_specs=placed,
        out_specs=(P(None, "heads", None), P(("ctx", "heads"), None)),
        check_vma=False,
    )
```

```python
import functools
import math

import jax
import jax.numpy as jnp
from jax import lax
from jax.experimental import pallas as pl
from jax.experimental.pallas import tpu as pltpu
from jax.sharding import PartitionSpec as P


F32 = jnp.float32
BF16 = jnp.bfloat16
LOG2E = math.log2(math.e)
SCORE_LOG2 = 192 ** (-0.5) * LOG2E
NEG = -1e30
LANES = 128
VMEM = pl.BlockSpec(memory_space=pltpu.VMEM)
HBM = pl.BlockSpec(memory_space=pltpu.HBM)
SMEM = pl.BlockSpec(memory_space=pltpu.SMEM)
CONTRACT_LAST = (((1,), (1,)), ((), ()))
QUAD = 4


def call(kernel, out_shape, in_specs, out_specs=None, scratch=(), flops=0, exps=0, nbytes=0):
    if out_specs is None:
        out_specs = jax.tree.map(lambda s: VMEM, out_shape)
    return pl.pallas_call(
        kernel,
        out_shape=out_shape,
        in_specs=in_specs,
        out_specs=out_specs,
        scratch_shapes=list(scratch),
        compiler_params=pltpu.CompilerParams(vmem_limit_bytes=40 << 20),
        cost_estimate=pl.CostEstimate(flops=flops, transcendentals=exps, bytes_accessed=nbytes),
    )


def half_at(core, half):
    return pl.ds(pl.multiple_of(core * half, LANES), half)


def head_sums(n_rows, n_heads, iq_ref, keys, w_ref, out_ref):
    rows = 256
    per = rows // n_heads
    for b in range(n_rows * n_heads // rows):
        dots = lax.dot_general(
            iq_ref[b * rows : (b + 1) * rows, :], keys, CONTRACT_LAST, preferred_element_type=F32
        )
        for i in range(per):
            row = b * per + i
            at = slice(row * n_heads, (row + 1) * n_heads)
            out_ref[row : row + 1, :] = jnp.sum(
                jnp.maximum(dots[i * n_heads : (i + 1) * n_heads, :], 0.0) * w_ref[at, 0:1],
                axis=0,
                keepdims=True,
            )


def logits_kernel(
    n_rows, n_heads, scale,
    pos_hbm, iq_hbm, ik_hbm, iw_hbm, lat_hbm,
    send_ref, bias_ref, iq_ref, ik_ref, w_ref, lat_ref, rows_ref,
    iw_ref, pos_ref, sems,
):
    half = send_ref.shape[1]
    copies = [
        pltpu.make_async_copy(a, b, sems.at[i])
        for i, (a, b) in enumerate(
            (
                (pos_hbm, pos_ref),
                (iw_hbm, iw_ref),
                (ik_hbm, ik_ref),
                (iq_hbm, iq_ref),
                (lat_hbm, lat_ref),
            )
        )
    ]
    for copy in copies:
        copy.start()
    copies[0].wait()
    start = lax.axis_index("ctx") * 2 * half
    count = jnp.int32(0)
    for seen in (True, False):
        for row in range(n_rows):
            rows_ref[count] = row
            count += ((pos_ref[row] >= start) == seen).astype(jnp.int32)
        if seen:
            visible = count
    rows_ref[n_rows + 1] = visible
    place = start + lax.broadcasted_iota(jnp.int32, (8, 2 * half), 1)
    sublane = lax.broadcasted_iota(jnp.int32, (8, 1), 0)
    for first in range(0, n_rows, 8):
        pos = jnp.zeros((8, 1), jnp.int32)
        for i in range(8):
            pos = jnp.where(sublane == i, pos_ref[first + i], pos)
        bias_ref[first : first + 8, :] = jnp.where(place <= pos, 0.0, NEG)
    copies[1].wait()
    for row in range(n_rows):
        w_ref[row * n_heads : (row + 1) * n_heads, :] = jnp.broadcast_to(
            iw_ref[:, row : row + 1] * scale, (n_heads, LANES)
        )
    copies[2].wait()
    copies[3].wait()
    core = lax.axis_index("heads") & 1
    head_sums(n_rows, n_heads, iq_ref, ik_ref[half_at(1 - core, half), :], w_ref, send_ref)
    copies[4].wait()


def kept_logits_kernel(
    n_rows, n_heads, bias_ref, iq_ref, ik_ref, w_ref, q_hbm, keep_ref, q_ref, sem
):
    copy = pltpu.make_async_copy(q_hbm.at[pl.ds(0, q_ref.shape[0]), :], q_ref, sem)
    copy.start()
    half = keep_ref.shape[1]
    core = lax.axis_index("heads") & 1
    head_sums(n_rows, n_heads, iq_ref, ik_ref[half_at(core, half), :], w_ref, keep_ref)
    keep_ref[...] += bias_ref[:, half_at(core, half)]
    copy.wait()


def scores_kernel(
    n_rows, n_heads, order_ref, bias_ref, q_ref, q_hbm, lat_ref, p_ref, stat_ref, s_even, s_odd, q_all, sems
):
    ready = q_ref.shape[0]
    rest = pl.ds(ready, q_all.shape[0] - ready)
    copies = (
        pltpu.make_async_copy(q_hbm.at[rest, :], q_all.at[rest, :], sems.at[0]),
        pltpu.make_async_copy(q_ref, q_all.at[pl.ds(0, ready), :], sems.at[1]),
    )
    for copy in copies:
        copy.start()
    block = s_even.shape[0]
    per = block // n_heads
    blocks = n_rows // per
    lane = lax.broadcasted_iota(jnp.int32, (n_heads, 2 * n_rows), 1)

    def scores(b, source):
        held = s_even if b % 2 == 0 else s_odd
        held[...] = jnp.dot(source, lat_ref[...], preferred_element_type=F32)

    def finish(b, i, bias, at):
        held = s_even if b % 2 == 0 else s_odd
        x = held[i * n_heads : (i + 1) * n_heads, :] + bias
        top = jnp.max(x, axis=1, keepdims=True)
        e = jnp.exp2((x - top) * SCORE_LOG2)
        p_ref[at, :] = e
        return top, jnp.sum(e, axis=1, keepdims=True)

    def all_rows():
        def source(b):
            first = b * block
            if first == ready:
                copies[0].wait()
            return (q_ref if first < ready else q_all)[first : first + block, :]

        scores(0, source(0))
        for b in range(blocks):
            if b + 1 < blocks:
                scores(b + 1, source(b + 1))
            for i in range(per):
                row = b * per + i
                at = slice(row * n_heads, (row + 1) * n_heads)
                top, total = finish(b, i, bias_ref[row : row + 1, :], at)
                stat_ref[:, row : row + 1] = top
                stat_ref[:, n_rows + row : n_rows + row + 1] = total
        copies[1].wait()

    def some_rows(n_blocks):
        for copy in copies:
            copy.wait()
        stats = jnp.where(lane < n_rows, NEG, 1.0)

        def place(row):
            return pl.ds(pl.multiple_of(row * n_heads, n_heads), n_heads)

        def source(b):
            rows = [order_ref[b * per + i] for i in range(per)]
            return jnp.concatenate([q_all[place(row), :] for row in rows], axis=0)

        scores(0, source(0))
        for b in range(n_blocks):
            if b + 1 < n_blocks:
                scores(b + 1, source(b + 1))
            for i in range(per):
                row = order_ref[b * per + i]
                top, total = finish(b, i, bias_ref[pl.ds(row, 1), :], place(row))
                stats = jnp.where(lane == row, top, jnp.where(lane == row + n_rows, total, stats))
        for i in range(n_blocks * per, n_rows):
            p_ref[place(order_ref[i]), :] = jnp.zeros((n_heads, p_ref.shape[1]), F32)
        stat_ref[...] = stats

    needed = (order_ref[n_rows + 1] + per - 1) // per
    sizes = range(2, blocks, 2)
    least = -1
    for size in sizes:
        pl.when((needed > least) & (needed <= size))(functools.partial(some_rows, size))
        least = size
    pl.when(needed > least)(all_rows)


def index_stats_kernel(mine_ref, other_ref, stat_ref, e_ref, out_ref, col):
    n_rows = mine_ref.shape[0]
    x = (mine_ref[...] + other_ref[...]) * LOG2E
    top = jnp.max(x, axis=1, keepdims=True)
    e = jnp.exp2(x - top)
    e_ref[...] = e
    col[:n_rows, 0:1] = top
    col[n_rows:, 0:1] = jnp.sum(e, axis=1, keepdims=True)
    n = stat_ref.shape[0] // 2
    size = stat_ref[:, :n_rows] * SCORE_LOG2 + jnp.log2(stat_ref[:, n_rows:])
    out_ref[:n, :n_rows] = size[:n, :]
    out_ref[:n, n_rows:] = size[n:, :]
    out_ref[n:, :] = jnp.transpose(col[...])[: out_ref.shape[0] - n, :]


def joined(stats):
    n = stats[0].shape[1] // 2
    tops = [s[:, :n] for s in stats]
    top = functools.reduce(jnp.maximum, tops)
    total = sum(s[:, n:] * jnp.exp2(t - top) for s, t in zip(stats, tops))
    return top, total


def target_sums(n_rows, n_heads, p_ref, weight, at, out_ref):
    for row in range(n_rows):
        out_ref[row : row + 1, :] = jnp.sum(
            p_ref[row * n_heads : (row + 1) * n_heads, at] * weight[:, row : row + 1],
            axis=0,
            keepdims=True,
        )


def target_kernel(n_rows, n_heads, all_ref, own_ref, p_ref, send_ref, weight_ref):
    half = send_ref.shape[1]
    n = all_ref.shape[0]
    some = n_heads // 2
    sizes = [all_ref[k, :some, :] for k in range(n)]
    top = functools.reduce(jnp.maximum, sizes)
    total = sum(jnp.exp2(s - top) for s in sizes)
    tops = own_ref[:, :n_rows] * SCORE_LOG2
    weight = jnp.concatenate(
        [
            jnp.exp2(tops[:some, :] - top[:, :n_rows]) / total[:, :n_rows],
            jnp.exp2(tops[some:, :] - top[:, n_rows:]) / total[:, n_rows:],
        ],
        axis=0,
    )
    peak, mass = joined([all_ref[k, some:, :] for k in range(n)])
    weight_ref[:n_heads, :n_rows] = weight
    for ref, first in ((weight_ref, n_heads), (send_ref, n_rows)):
        ref[first:, :n_rows] = peak
        ref[first:, n_rows : 2 * n_rows] = mass
    core = lax.axis_index("heads") & 1
    target_sums(n_rows, n_heads, p_ref, weight, half_at(1 - core, half), send_ref)


def kept_target_kernel(n_rows, n_heads, weight_ref, p_ref, keep_ref):
    core = lax.axis_index("heads") & 1
    at = half_at(core, keep_ref.shape[1])
    target_sums(n_rows, n_heads, p_ref, weight_ref[:n_heads, :n_rows], at, keep_ref)


def probs_kernel(mine_ref, other_ref, own_ref, e_ref, prob_ref, col):
    n_rows = e_ref.shape[0]
    first = mine_ref.shape[0] - 8
    peak, mass = joined([mine_ref[first:, :], other_ref[n_rows:, : 2 * n_rows]])
    factor = jnp.exp2(own_ref[own_ref.shape[0] - 8 :, :n_rows] - peak) / mass
    col[:8, :n_rows] = factor
    prob_ref[...] = e_ref[...] * jnp.transpose(col[...])[:n_rows, 0:1]


def mask_kernel(iq_ref, ik_ref, w_ref, wm_ref, iqt_ref):
    rows = 256
    for b in range(iq_ref.shape[0] // rows):
        at = slice(b * rows, (b + 1) * rows)
        dots = lax.dot_general(iq_ref[at, :], ik_ref[...], CONTRACT_LAST, preferred_element_type=F32)
        wm_ref[at, :] = jnp.where(dots > 0.0, w_ref[at, 0:1], 0.0)
        iqt_ref[:, at] = jnp.transpose(iq_ref[at, :])


def coefficients(n_heads, g_rows, wm):
    n = g_rows.shape[1]
    g = jnp.concatenate(
        [jnp.broadcast_to(g_rows[i : i + 1, :], (n_heads, n)) for i in range(g_rows.shape[0])], axis=0
    )
    return (g * wm).astype(BF16)


def own_grads_kernel(n_heads, g_ref, wm_ref, iqt_ref, ik_ref, gq_ref, gkt_ref):
    half = g_ref.shape[1]
    at = half_at(lax.axis_index("heads") & 1, half)
    rows = 256
    per = rows // n_heads
    for b in range(wm_ref.shape[0] // rows):
        row = slice(b * rows, (b + 1) * rows)
        coef = coefficients(n_heads, g_ref[b * per : (b + 1) * per, :], wm_ref[row, at])
        gq_ref[row, :] = jnp.dot(coef, ik_ref[at, :], preferred_element_type=F32)
        term = jnp.dot(iqt_ref[:, row], coef, preferred_element_type=F32)
        if b == 0:
            gkt_ref[...] = term
        else:
            gkt_ref[...] += term


def other_grads_kernel(n_heads, k, g_ref, wm_ref, iqt_ref, ik_ref, gq_ref, *rest):
    *acc_ref, out_ref, gkt_ref = rest
    half = g_ref.shape[1]
    at = half_at(1 - (lax.axis_index("heads") & 1), half)
    rows = out_ref.shape[0]
    per = rows // n_heads
    block = (lax.axis_index("ctx") & (QUAD - 1)) ^ k
    row = pl.ds(pl.multiple_of(block * rows, rows), rows)
    coef = coefficients(
        n_heads, g_ref[pl.ds(pl.multiple_of(block * per, per), per), :], wm_ref[row, at]
    )
    out_ref[...] = gq_ref[row, :] + jnp.dot(coef, ik_ref[at, :], preferred_element_type=F32)
    term = jnp.dot(iqt_ref[:, row], coef, preferred_element_type=F32)
    gkt_ref[...] = acc_ref[0][...] + term if acc_ref else term


def key_grads_kernel(mine_ref, other_ref, *rest):
    *gk_refs, gk_t = rest
    half = mine_ref.shape[1]
    me = lax.axis_index("heads")
    gk_t[:, half_at(me & 1, half)] = mine_ref[...]
    gk_t[:, half_at(1 - (me & 1), half)] = other_ref[...]
    size = gk_refs[0].shape[0]
    for k, ref in enumerate(gk_refs):
        at = pl.multiple_of((me ^ k) * size, LANES)
        ref[...] = jnp.transpose(gk_t[:, pl.ds(at, size)])


def outputs_kernel(n_quad, *refs):
    *in_refs, gq_hbm, gk_hbm, total, sems = refs
    blocks, parts = in_refs[:n_quad], in_refs[n_quad:]
    size = blocks[0].shape[0]
    slot = lax.axis_index("ctx") & (n_quad - 1)
    copies = [
        pltpu.make_async_copy(
            ref, gq_hbm.at[pl.ds(pl.multiple_of((slot ^ k) * size, size), size), :], sems.at[k]
        )
        for k, ref in enumerate(blocks)
    ]
    for copy in copies:
        copy.start()
    total[...] = sum(ref[...] for ref in parts)
    last = pltpu.make_async_copy(total, gk_hbm, sems.at[n_quad])
    last.start()
    for copy in copies + [last]:
        copy.wait()


def body(queries, latents, index_queries, index_keys, index_weights, positions):
    n_rows, heads_local, width = queries.shape
    keys = latents.shape[0]
    index_local, depth = index_queries.shape[1:]
    n_ctx = lax.axis_size("ctx")
    n_heads = lax.axis_size("heads")
    half = keys // 2
    loss_scale = float(n_ctx * keys // 64)
    shape = jax.ShapeDtypeStruct

    def swapped(value, axis, k):
        n = lax.axis_size(axis)
        return lax.ppermute(value, axis, [(i, i ^ k) for i in range(n)])

    flat = (n_rows * index_local, depth)
    send, bias, iq, ik, w, lat, order = call(
        functools.partial(
            logits_kernel, n_rows, index_local, (index_local * n_heads * depth) ** (-0.5)
        ),
        (
            shape((n_rows, half), F32),
            shape((n_rows, keys), F32),
            shape(flat, BF16),
            shape((keys, depth), BF16),
            shape((flat[0], LANES), F32),
            shape((width, keys), BF16),
            shape((n_rows + 8,), jnp.int32),
        ),
        [HBM] * 5,
        out_specs=(VMEM,) * 6 + (SMEM,),
        scratch=[
            pltpu.VMEM((index_local, n_rows), F32),
            pltpu.SMEM((n_rows,), jnp.int32),
            pltpu.SemaphoreType.DMA((5,)),
        ],
        flops=flat[0] * depth * keys,
        nbytes=latents.size * 2,
    )(
        *(
            pltpu.with_memory_space_constraint(x, pltpu.HBM)
            for x in (
                positions,
                index_queries.reshape(flat),
                index_keys,
                index_weights.T,
                latents.T,
            )
        )
    )
    got = swapped(send, "heads", 1)
    flat_queries = pltpu.with_memory_space_constraint(
        queries.reshape(n_rows * heads_local, width), pltpu.HBM
    )
    ready = n_rows * heads_local // 4
    keep, q = call(
        functools.partial(kept_logits_kernel, n_rows, index_local),
        (shape((n_rows, half), F32), shape((ready, width), BF16)),
        [VMEM] * 4 + [HBM],
        scratch=[pltpu.SemaphoreType.DMA],
        flops=flat[0] * depth * keys,
        nbytes=queries.size * 2,
    )(bias, iq, ik, w, flat_queries)
    logit_mine = keep + got
    logit_other = swapped(logit_mine, "heads", 2)
    probs, stats = call(
        functools.partial(scores_kernel, n_rows, heads_local),
        (shape((n_rows * heads_local, keys), F32), shape((heads_local, 2 * n_rows), F32)),
        [SMEM, VMEM, VMEM, HBM, VMEM],
        scratch=[pltpu.VMEM((256, keys), F32)] * 2
        + [pltpu.VMEM(flat_queries.shape, BF16), pltpu.SemaphoreType.DMA((2,))],
        flops=2 * queries.size * keys,
        exps=n_rows * heads_local * keys,
        nbytes=queries.size * 2,
    )(order, bias, q, flat_queries, lat)
    exps, sizes = call(
        index_stats_kernel,
        (shape((n_rows, half), F32), shape((heads_local // 2 + 8, 2 * n_rows), F32)),
        [VMEM] * 3,
        scratch=[pltpu.VMEM((LANES, LANES), F32)],
    )(logit_mine, logit_other, stats)
    everyone = lax.all_to_all(jnp.broadcast_to(sizes, (n_ctx,) + sizes.shape), "ctx", 0, 0)
    send, weight = call(
        functools.partial(target_kernel, n_rows, heads_local),
        (shape((n_rows + 8, half), F32), shape((heads_local + 8, 2 * n_rows), F32)),
        [VMEM] * 3,
        flops=n_rows * heads_local * keys,
    )(everyone, stats, probs)
    got = swapped(send, "heads", 1)
    keep = call(
        functools.partial(kept_target_kernel, n_rows, heads_local),
        shape((n_rows, half), F32),
        [VMEM] * 2,
        flops=n_rows * heads_local * keys,
    )(weight, probs)
    index_probs = call(
        probs_kernel,
        shape((n_rows, half), F32),
        [VMEM] * 4,
        scratch=[pltpu.VMEM((LANES, LANES), F32)],
    )(weight, got, sizes, exps)
    target = keep + got[:n_rows]
    masked, iq_t = call(
        mask_kernel,
        (shape((flat[0], keys), F32), shape(flat[::-1], BF16)),
        [VMEM] * 3,
        flops=2 * flat[0] * depth * keys,
    )(iq, ik, w)
    rest, masked, iq_t = lax.optimization_barrier((swapped(target, "heads", 2), masked, iq_t))
    target = target + rest
    grad = loss_scale * (index_probs - target * (1.0 / (heads_local * n_heads)))
    grad_other = swapped(grad, "heads", 1)
    query_sums, key_sums = call(
        functools.partial(own_grads_kernel, index_local),
        (shape(flat, F32), shape((depth, half), F32)),
        [VMEM] * 4,
        flops=2 * flat[0] * depth * keys,
    )(grad, masked, iq_t, ik)
    query_parts = [None] * QUAD
    sums = ()
    for k in range(QUAD - 1, -1, -1):
        query_parts[k], more = call(
            functools.partial(other_grads_kernel, index_local, k),
            (shape((flat[0] // QUAD, depth), F32), shape((depth, half), F32)),
            [VMEM] * (5 + len(sums)),
            flops=2 * flat[0] * depth * keys // QUAD,
        )(grad_other, masked, iq_t, ik, query_sums, *sums)
        sums = (more,)
        if k:
            query_parts[k] = swapped(query_parts[k], "ctx", k)
    owned = keys // n_heads
    key_parts = call(
        key_grads_kernel,
        (shape((owned, depth), F32),) * n_heads,
        [VMEM] * 2,
        scratch=[pltpu.VMEM((depth, keys), F32)],
    )(key_sums, *sums)
    mine = sum(query_parts)
    key_parts = [key_parts[0]] + [swapped(key_parts[k], "heads", k) for k in range(1, n_heads)]
    k = QUAD
    while k < n_ctx:
        mine = mine + swapped(mine, "ctx", k)
        k *= 2
    blocks = [mine]
    for k in range(1, QUAD):
        blocks.append(swapped(mine, "ctx", k))
    grad_queries, grad_keys = call(
        functools.partial(outputs_kernel, QUAD),
        (shape(flat, F32), shape((owned, depth), F32)),
        [VMEM] * (QUAD + n_heads),
        out_specs=(HBM, HBM),
        scratch=[pltpu.VMEM((owned, depth), F32), pltpu.SemaphoreType.DMA((QUAD + 1,))],
    )(*blocks, *key_parts)
    return grad_queries.reshape(n_rows, index_local, depth), grad_keys


def solution(mesh):
    placed = (
        P(None, "heads", None),
        P("ctx", None),
        P(None, "heads", None),
        P("ctx", None),
        P(None, "heads"),
        P(),
    )
    return jax.shard_map(
        body,
        mesh=mesh,
        in_specs=placed,
        out_specs=(P(None, "heads", None), P(("ctx", "heads"), None)),
        check_vma=False,
    )
```

```python
import functools
import math

import jax
import jax.numpy as jnp
from jax import lax
from jax.experimental import pallas as pl
from jax.experimental.pallas import tpu as pltpu
from jax.sharding import PartitionSpec as P


F32 = jnp.float32
BF16 = jnp.bfloat16
LOG2E = math.log2(math.e)
SCORE_LOG2 = 192 ** (-0.5) * LOG2E
NEG = -1e30
LANES = 128
VMEM = pl.BlockSpec(memory_space=pltpu.VMEM)
HBM = pl.BlockSpec(memory_space=pltpu.HBM)
SMEM = pl.BlockSpec(memory_space=pltpu.SMEM)
CONTRACT_LAST = (((1,), (1,)), ((), ()))
QUAD = 4


def call(kernel, out_shape, in_specs, out_specs=None, scratch=(), flops=0, exps=0, nbytes=0):
    if out_specs is None:
        out_specs = jax.tree.map(lambda s: VMEM, out_shape)
    return pl.pallas_call(
        kernel,
        out_shape=out_shape,
        in_specs=in_specs,
        out_specs=out_specs,
        scratch_shapes=list(scratch),
        compiler_params=pltpu.CompilerParams(vmem_limit_bytes=40 << 20),
        cost_estimate=pl.CostEstimate(flops=flops, transcendentals=exps, bytes_accessed=nbytes),
    )


def half_at(core, half):
    return pl.ds(pl.multiple_of(core * half, LANES), half)


def head_sums(n_rows, n_heads, iq_ref, keys, w_ref, out_ref):
    rows = 256
    per = rows // n_heads
    for b in range(n_rows * n_heads // rows):
        dots = lax.dot_general(
            iq_ref[b * rows : (b + 1) * rows, :], keys, CONTRACT_LAST, preferred_element_type=F32
        )
        for i in range(per):
            row = b * per + i
            at = slice(row * n_heads, (row + 1) * n_heads)
            out_ref[row : row + 1, :] = jnp.sum(
                jnp.maximum(dots[i * n_heads : (i + 1) * n_heads, :], 0.0) * w_ref[at, 0:1],
                axis=0,
                keepdims=True,
            )


def logits_kernel(
    n_rows, n_heads, scale,
    pos_hbm, iq_hbm, ik_hbm, iw_hbm, lat_hbm,
    send_ref, bias_ref, iq_ref, ik_ref, w_ref, lat_ref, rows_ref,
    iw_ref, pos_ref, sems,
):
    half = send_ref.shape[1]
    copies = [
        pltpu.make_async_copy(a, b, sems.at[i])
        for i, (a, b) in enumerate(
            (
                (pos_hbm, pos_ref),
                (iw_hbm, iw_ref),
                (ik_hbm, ik_ref),
                (iq_hbm, iq_ref),
                (lat_hbm, lat_ref),
            )
        )
    ]
    for copy in copies:
        copy.start()
    copies[0].wait()
    start = lax.axis_index("ctx") * 2 * half
    for row in range(n_rows):
        rows_ref[row] = 0
    count = jnp.int32(0)
    for row in range(n_rows):
        rows_ref[count] = row
        count += (pos_ref[row] >= start).astype(jnp.int32)
    rows_ref[n_rows + 1] = count
    place = start + lax.broadcasted_iota(jnp.int32, (8, 2 * half), 1)
    sublane = lax.broadcasted_iota(jnp.int32, (8, 1), 0)
    for first in range(0, n_rows, 8):
        pos = jnp.zeros((8, 1), jnp.int32)
        for i in range(8):
            pos = jnp.where(sublane == i, pos_ref[first + i], pos)
        bias_ref[first : first + 8, :] = jnp.where(place <= pos, 0.0, NEG)
    copies[1].wait()
    for row in range(n_rows):
        w_ref[row * n_heads : (row + 1) * n_heads, :] = jnp.broadcast_to(
            iw_ref[:, row : row + 1] * scale, (n_heads, LANES)
        )
    copies[2].wait()
    copies[3].wait()
    core = lax.axis_index("heads") & 1
    head_sums(n_rows, n_heads, iq_ref, ik_ref[half_at(1 - core, half), :], w_ref, send_ref)
    copies[4].wait()


def kept_logits_kernel(
    n_rows, n_heads, bias_ref, iq_ref, ik_ref, w_ref, q_hbm, keep_ref, q_ref, sem
):
    copy = pltpu.make_async_copy(q_hbm.at[pl.ds(0, q_ref.shape[0]), :], q_ref, sem)
    copy.start()
    half = keep_ref.shape[1]
    core = lax.axis_index("heads") & 1
    head_sums(n_rows, n_heads, iq_ref, ik_ref[half_at(core, half), :], w_ref, keep_ref)
    keep_ref[...] += bias_ref[:, half_at(core, half)]
    copy.wait()


def scores_kernel(
    n_rows, n_heads, order_ref, bias_ref, q_ref, q_hbm, lat_ref, p_ref, stat_ref, s_even, s_odd, q_all, sems
):
    ready = q_ref.shape[0]
    rest = pl.ds(ready, q_all.shape[0] - ready)
    copies = (
        pltpu.make_async_copy(q_hbm.at[rest, :], q_all.at[rest, :], sems.at[0]),
        pltpu.make_async_copy(q_ref, q_all.at[pl.ds(0, ready), :], sems.at[1]),
    )
    for copy in copies:
        copy.start()
    block = s_even.shape[0]
    per = block // n_heads
    blocks = n_rows // per
    lane = lax.broadcasted_iota(jnp.int32, (n_heads, 2 * n_rows), 1)

    def scores(b, source):
        held = s_even if b % 2 == 0 else s_odd
        held[...] = jnp.dot(source, lat_ref[...], preferred_element_type=F32)

    def finish(b, i, bias, at):
        held = s_even if b % 2 == 0 else s_odd
        x = held[i * n_heads : (i + 1) * n_heads, :] + bias
        top = jnp.max(x, axis=1, keepdims=True)
        e = jnp.exp2((x - top) * SCORE_LOG2)
        p_ref[at, :] = e
        return top, jnp.sum(e, axis=1, keepdims=True)

    def all_rows():
        def source(b):
            first = b * block
            if first == ready:
                copies[0].wait()
            return (q_ref if first < ready else q_all)[first : first + block, :]

        scores(0, source(0))
        for b in range(blocks):
            if b + 1 < blocks:
                scores(b + 1, source(b + 1))
            for i in range(per):
                row = b * per + i
                at = slice(row * n_heads, (row + 1) * n_heads)
                top, total = finish(b, i, bias_ref[row : row + 1, :], at)
                stat_ref[:, row : row + 1] = top
                stat_ref[:, n_rows + row : n_rows + row + 1] = total
        copies[1].wait()

    def some_rows(n_blocks):
        for row in range(n_rows):
            at = slice(row * n_heads, (row + 1) * n_heads)
            p_ref[at, :] = jnp.zeros((n_heads, p_ref.shape[1]), F32)
        for copy in copies:
            copy.wait()
        stats = jnp.where(lane < n_rows, NEG, 1.0)

        def place(row):
            return pl.ds(pl.multiple_of(row * n_heads, n_heads), n_heads)

        def source(b):
            rows = [order_ref[b * per + i] for i in range(per)]
            return jnp.concatenate([q_all[place(row), :] for row in rows], axis=0)

        scores(0, source(0))
        for b in range(n_blocks):
            if b + 1 < n_blocks:
                scores(b + 1, source(b + 1))
            for i in range(per):
                row = order_ref[b * per + i]
                top, total = finish(b, i, bias_ref[pl.ds(row, 1), :], place(row))
                stats = jnp.where(lane == row, top, jnp.where(lane == row + n_rows, total, stats))
        stat_ref[...] = stats

    needed = (order_ref[n_rows + 1] + per - 1) // per
    sizes = range(2, blocks, 2)
    least = -1
    for size in sizes:
        pl.when((needed > least) & (needed <= size))(functools.partial(some_rows, size))
        least = size
    pl.when(needed > least)(all_rows)


def index_stats_kernel(mine_ref, other_ref, stat_ref, e_ref, out_ref, col):
    n_rows = mine_ref.shape[0]
    x = (mine_ref[...] + other_ref[...]) * LOG2E
    top = jnp.max(x, axis=1, keepdims=True)
    e = jnp.exp2(x - top)
    e_ref[...] = e
    col[:n_rows, 0:1] = top
    col[n_rows:, 0:1] = jnp.sum(e, axis=1, keepdims=True)
    n = stat_ref.shape[0] // 2
    size = stat_ref[:, :n_rows] * SCORE_LOG2 + jnp.log2(stat_ref[:, n_rows:])
    out_ref[:n, :n_rows] = size[:n, :]
    out_ref[:n, n_rows:] = size[n:, :]
    out_ref[n:, :] = jnp.transpose(col[...])[: out_ref.shape[0] - n, :]


def joined(stats):
    n = stats[0].shape[1] // 2
    tops = [s[:, :n] for s in stats]
    top = functools.reduce(jnp.maximum, tops)
    total = sum(s[:, n:] * jnp.exp2(t - top) for s, t in zip(stats, tops))
    return top, total


def target_sums(n_rows, n_heads, p_ref, weight, at, out_ref):
    for row in range(n_rows):
        out_ref[row : row + 1, :] = jnp.sum(
            p_ref[row * n_heads : (row + 1) * n_heads, at] * weight[:, row : row + 1],
            axis=0,
            keepdims=True,
        )


def target_kernel(n_rows, n_heads, all_ref, own_ref, p_ref, send_ref, weight_ref):
    half = send_ref.shape[1]
    n = all_ref.shape[0]
    some = n_heads // 2
    sizes = [all_ref[k, :some, :] for k in range(n)]
    top = functools.reduce(jnp.maximum, sizes)
    total = sum(jnp.exp2(s - top) for s in sizes)
    tops = own_ref[:, :n_rows] * SCORE_LOG2
    weight = jnp.concatenate(
        [
            jnp.exp2(tops[:some, :] - top[:, :n_rows]) / total[:, :n_rows],
            jnp.exp2(tops[some:, :] - top[:, n_rows:]) / total[:, n_rows:],
        ],
        axis=0,
    )
    peak, mass = joined([all_ref[k, some:, :] for k in range(n)])
    weight_ref[:n_heads, :n_rows] = weight
    for ref, first in ((weight_ref, n_heads), (send_ref, n_rows)):
        ref[first:, :n_rows] = peak
        ref[first:, n_rows : 2 * n_rows] = mass
    core = lax.axis_index("heads") & 1
    target_sums(n_rows, n_heads, p_ref, weight, half_at(1 - core, half), send_ref)


def kept_target_kernel(n_rows, n_heads, weight_ref, p_ref, keep_ref):
    core = lax.axis_index("heads") & 1
    at = half_at(core, keep_ref.shape[1])
    target_sums(n_rows, n_heads, p_ref, weight_ref[:n_heads, :n_rows], at, keep_ref)


def probs_kernel(mine_ref, other_ref, own_ref, e_ref, prob_ref, col):
    n_rows = e_ref.shape[0]
    first = mine_ref.shape[0] - 8
    peak, mass = joined([mine_ref[first:, :], other_ref[n_rows:, : 2 * n_rows]])
    factor = jnp.exp2(own_ref[own_ref.shape[0] - 8 :, :n_rows] - peak) / mass
    col[:8, :n_rows] = factor
    prob_ref[...] = e_ref[...] * jnp.transpose(col[...])[:n_rows, 0:1]


def mask_kernel(iq_ref, ik_ref, w_ref, wm_ref, iqt_ref):
    rows = 256
    for b in range(iq_ref.shape[0] // rows):
        at = slice(b * rows, (b + 1) * rows)
        dots = lax.dot_general(iq_ref[at, :], ik_ref[...], CONTRACT_LAST, preferred_element_type=F32)
        wm_ref[at, :] = jnp.where(dots > 0.0, w_ref[at, 0:1], 0.0)
        iqt_ref[:, at] = jnp.transpose(iq_ref[at, :])


def coefficients(n_heads, g_rows, wm):
    n = g_rows.shape[1]
    g = jnp.concatenate(
        [jnp.broadcast_to(g_rows[i : i + 1, :], (n_heads, n)) for i in range(g_rows.shape[0])], axis=0
    )
    return (g * wm).astype(BF16)


def own_grads_kernel(n_heads, g_ref, wm_ref, iqt_ref, ik_ref, gq_ref, gkt_ref):
    half = g_ref.shape[1]
    at = half_at(lax.axis_index("heads") & 1, half)
    rows = 256
    per = rows // n_heads
    for b in range(wm_ref.shape[0] // rows):
        row = slice(b * rows, (b + 1) * rows)
        coef = coefficients(n_heads, g_ref[b * per : (b + 1) * per, :], wm_ref[row, at])
        gq_ref[row, :] = jnp.dot(coef, ik_ref[at, :], preferred_element_type=F32)
        term = jnp.dot(iqt_ref[:, row], coef, preferred_element_type=F32)
        if b == 0:
            gkt_ref[...] = term
        else:
            gkt_ref[...] += term


def other_grads_kernel(n_heads, k, g_ref, wm_ref, iqt_ref, ik_ref, gq_ref, *rest):
    *acc_ref, out_ref, gkt_ref = rest
    half = g_ref.shape[1]
    at = half_at(1 - (lax.axis_index("heads") & 1), half)
    rows = out_ref.shape[0]
    per = rows // n_heads
    block = (lax.axis_index("ctx") & (QUAD - 1)) ^ k
    row = pl.ds(pl.multiple_of(block * rows, rows), rows)
    coef = coefficients(
        n_heads, g_ref[pl.ds(pl.multiple_of(block * per, per), per), :], wm_ref[row, at]
    )
    out_ref[...] = gq_ref[row, :] + jnp.dot(coef, ik_ref[at, :], preferred_element_type=F32)
    term = jnp.dot(iqt_ref[:, row], coef, preferred_element_type=F32)
    gkt_ref[...] = acc_ref[0][...] + term if acc_ref else term


def key_grads_kernel(mine_ref, other_ref, *rest):
    *gk_refs, gk_t = rest
    half = mine_ref.shape[1]
    me = lax.axis_index("heads")
    gk_t[:, half_at(me & 1, half)] = mine_ref[...]
    gk_t[:, half_at(1 - (me & 1), half)] = other_ref[...]
    size = gk_refs[0].shape[0]
    for k, ref in enumerate(gk_refs):
        at = pl.multiple_of((me ^ k) * size, LANES)
        ref[...] = jnp.transpose(gk_t[:, pl.ds(at, size)])


def outputs_kernel(n_quad, *refs):
    *in_refs, gq_hbm, gk_hbm, total, sems = refs
    blocks, parts = in_refs[:n_quad], in_refs[n_quad:]
    size = blocks[0].shape[0]
    slot = lax.axis_index("ctx") & (n_quad - 1)
    copies = [
        pltpu.make_async_copy(
            ref, gq_hbm.at[pl.ds(pl.multiple_of((slot ^ k) * size, size), size), :], sems.at[k]
        )
        for k, ref in enumerate(blocks)
    ]
    for copy in copies:
        copy.start()
    total[...] = sum(ref[...] for ref in parts)
    last = pltpu.make_async_copy(total, gk_hbm, sems.at[n_quad])
    last.start()
    for copy in copies + [last]:
        copy.wait()


def body(queries, latents, index_queries, index_keys, index_weights, positions):
    n_rows, heads_local, width = queries.shape
    keys = latents.shape[0]
    index_local, depth = index_queries.shape[1:]
    n_ctx = lax.axis_size("ctx")
    n_heads = lax.axis_size("heads")
    half = keys // 2
    loss_scale = float(n_ctx * keys // 64)
    shape = jax.ShapeDtypeStruct

    def swapped(value, axis, k):
        n = lax.axis_size(axis)
        return lax.ppermute(value, axis, [(i, i ^ k) for i in range(n)])

    flat = (n_rows * index_local, depth)
    send, bias, iq, ik, w, lat, order = call(
        functools.partial(
            logits_kernel, n_rows, index_local, (index_local * n_heads * depth) ** (-0.5)
        ),
        (
            shape((n_rows, half), F32),
            shape((n_rows, keys), F32),
            shape(flat, BF16),
            shape((keys, depth), BF16),
            shape((flat[0], LANES), F32),
            shape((width, keys), BF16),
            shape((n_rows + 8,), jnp.int32),
        ),
        [HBM] * 5,
        out_specs=(VMEM,) * 6 + (SMEM,),
        scratch=[
            pltpu.VMEM((index_local, n_rows), F32),
            pltpu.SMEM((n_rows,), jnp.int32),
            pltpu.SemaphoreType.DMA((5,)),
        ],
        flops=flat[0] * depth * keys,
        nbytes=latents.size * 2,
    )(
        *(
            pltpu.with_memory_space_constraint(x, pltpu.HBM)
            for x in (
                positions,
                index_queries.reshape(flat),
                index_keys,
                index_weights.T,
                latents.T,
            )
        )
    )
    got = swapped(send, "heads", 1)
    flat_queries = pltpu.with_memory_space_constraint(
        queries.reshape(n_rows * heads_local, width), pltpu.HBM
    )
    ready = n_rows * heads_local // 2
    keep, q = call(
        functools.partial(kept_logits_kernel, n_rows, index_local),
        (shape((n_rows, half), F32), shape((ready, width), BF16)),
        [VMEM] * 4 + [HBM],
        scratch=[pltpu.SemaphoreType.DMA],
        flops=flat[0] * depth * keys,
        nbytes=queries.size * 2,
    )(bias, iq, ik, w, flat_queries)
    logit_mine = keep + got
    logit_other = swapped(logit_mine, "heads", 2)
    probs, stats = call(
        functools.partial(scores_kernel, n_rows, heads_local),
        (shape((n_rows * heads_local, keys), F32), shape((heads_local, 2 * n_rows), F32)),
        [SMEM, VMEM, VMEM, HBM, VMEM],
        scratch=[pltpu.VMEM((256, keys), F32)] * 2
        + [pltpu.VMEM(flat_queries.shape, BF16), pltpu.SemaphoreType.DMA((2,))],
        flops=2 * queries.size * keys,
        exps=n_rows * heads_local * keys,
        nbytes=queries.size * 2,
    )(order, bias, q, flat_queries, lat)
    exps, sizes = call(
        index_stats_kernel,
        (shape((n_rows, half), F32), shape((heads_local // 2 + 8, 2 * n_rows), F32)),
        [VMEM] * 3,
        scratch=[pltpu.VMEM((LANES, LANES), F32)],
    )(logit_mine, logit_other, stats)
    everyone = lax.all_to_all(jnp.broadcast_to(sizes, (n_ctx,) + sizes.shape), "ctx", 0, 0)
    send, weight = call(
        functools.partial(target_kernel, n_rows, heads_local),
        (shape((n_rows + 8, half), F32), shape((heads_local + 8, 2 * n_rows), F32)),
        [VMEM] * 3,
        flops=n_rows * heads_local * keys,
    )(everyone, stats, probs)
    got = swapped(send, "heads", 1)
    keep = call(
        functools.partial(kept_target_kernel, n_rows, heads_local),
        shape((n_rows, half), F32),
        [VMEM] * 2,
        flops=n_rows * heads_local * keys,
    )(weight, probs)
    index_probs = call(
        probs_kernel,
        shape((n_rows, half), F32),
        [VMEM] * 4,
        scratch=[pltpu.VMEM((LANES, LANES), F32)],
    )(weight, got, sizes, exps)
    target = keep + got[:n_rows]
    masked, iq_t = call(
        mask_kernel,
        (shape((flat[0], keys), F32), shape(flat[::-1], BF16)),
        [VMEM] * 3,
        flops=2 * flat[0] * depth * keys,
    )(iq, ik, w)
    rest, masked, iq_t = lax.optimization_barrier((swapped(target, "heads", 2), masked, iq_t))
    target = target + rest
    grad = loss_scale * (index_probs - target * (1.0 / (heads_local * n_heads)))
    grad_other = swapped(grad, "heads", 1)
    query_sums, key_sums = call(
        functools.partial(own_grads_kernel, index_local),
        (shape(flat, F32), shape((depth, half), F32)),
        [VMEM] * 4,
        flops=2 * flat[0] * depth * keys,
    )(grad, masked, iq_t, ik)
    query_parts = [None] * QUAD
    sums = ()
    for k in range(QUAD - 1, -1, -1):
        query_parts[k], more = call(
            functools.partial(other_grads_kernel, index_local, k),
            (shape((flat[0] // QUAD, depth), F32), shape((depth, half), F32)),
            [VMEM] * (5 + len(sums)),
            flops=2 * flat[0] * depth * keys // QUAD,
        )(grad_other, masked, iq_t, ik, query_sums, *sums)
        sums = (more,)
        if k:
            query_parts[k] = swapped(query_parts[k], "ctx", k)
    owned = keys // n_heads
    key_parts = call(
        key_grads_kernel,
        (shape((owned, depth), F32),) * n_heads,
        [VMEM] * 2,
        scratch=[pltpu.VMEM((depth, keys), F32)],
    )(key_sums, *sums)
    mine = sum(query_parts)
    key_parts = [key_parts[0]] + [swapped(key_parts[k], "heads", k) for k in range(1, n_heads)]
    k = QUAD
    while k < n_ctx:
        mine = mine + swapped(mine, "ctx", k)
        k *= 2
    blocks = [mine]
    for k in range(1, QUAD):
        blocks.append(swapped(mine, "ctx", k))
    grad_queries, grad_keys = call(
        functools.partial(outputs_kernel, QUAD),
        (shape(flat, F32), shape((owned, depth), F32)),
        [VMEM] * (QUAD + n_heads),
        out_specs=(HBM, HBM),
        scratch=[pltpu.VMEM((owned, depth), F32), pltpu.SemaphoreType.DMA((QUAD + 1,))],
    )(*blocks, *key_parts)
    return grad_queries.reshape(n_rows, index_local, depth), grad_keys


def solution(mesh):
    placed = (
        P(None, "heads", None),
        P("ctx", None),
        P(None, "heads", None),
        P("ctx", None),
        P(None, "heads"),
        P(),
    )
    return jax.shard_map(
        body,
        mesh=mesh,
        in_specs=placed,
        out_specs=(P(None, "heads", None), P(("ctx", "heads"), None)),
        check_vma=False,
    )
```

```python
import functools
import math

import jax
import jax.numpy as jnp
from jax import lax
from jax.experimental import pallas as pl
from jax.experimental.pallas import tpu as pltpu
from jax.sharding import PartitionSpec as P


F32 = jnp.float32
BF16 = jnp.bfloat16
LOG2E = math.log2(math.e)
SCORE_LOG2 = 192 ** (-0.5) * LOG2E
NEG = -1e30
LANES = 128
VMEM = pl.BlockSpec(memory_space=pltpu.VMEM)
HBM = pl.BlockSpec(memory_space=pltpu.HBM)
CONTRACT_LAST = (((1,), (1,)), ((), ()))
QUAD = 4


def call(kernel, out_shape, in_specs, out_specs=None, scratch=(), flops=0, exps=0, nbytes=0):
    if out_specs is None:
        out_specs = jax.tree.map(lambda s: VMEM, out_shape)
    return pl.pallas_call(
        kernel,
        out_shape=out_shape,
        in_specs=in_specs,
        out_specs=out_specs,
        scratch_shapes=list(scratch),
        compiler_params=pltpu.CompilerParams(vmem_limit_bytes=40 << 20),
        cost_estimate=pl.CostEstimate(flops=flops, transcendentals=exps, bytes_accessed=nbytes),
    )


def half_at(core, half):
    return pl.ds(pl.multiple_of(core * half, LANES), half)


def head_sums(n_rows, n_heads, iq_ref, keys, w_ref, out_ref):
    rows = 256
    per = rows // n_heads
    for b in range(n_rows * n_heads // rows):
        dots = lax.dot_general(
            iq_ref[b * rows : (b + 1) * rows, :], keys, CONTRACT_LAST, preferred_element_type=F32
        )
        for i in range(per):
            row = b * per + i
            out_ref[row : row + 1, :] = jnp.sum(
                jnp.maximum(dots[i * n_heads : (i + 1) * n_heads, :], 0.0) * w_ref[:, row : row + 1],
                axis=0,
                keepdims=True,
            )


def logits_kernel(
    n_rows, n_heads, scale,
    pos_hbm, iq_hbm, ik_hbm, iw_hbm, lat_hbm,
    send_ref, bias_ref, iq_ref, ik_ref, w_ref, lat_ref,
    iw_ref, pos_ref, sems,
):
    half = send_ref.shape[1]
    copies = [
        pltpu.make_async_copy(a, b, sems.at[i])
        for i, (a, b) in enumerate(
            (
                (pos_hbm, pos_ref),
                (iw_hbm, iw_ref),
                (ik_hbm, ik_ref),
                (iq_hbm, iq_ref),
                (lat_hbm, lat_ref),
            )
        )
    ]
    for copy in copies:
        copy.start()
    copies[0].wait()
    place = lax.axis_index("ctx") * 2 * half + lax.broadcasted_iota(jnp.int32, (8, 2 * half), 1)
    sublane = lax.broadcasted_iota(jnp.int32, (8, 1), 0)
    for first in range(0, n_rows, 8):
        pos = jnp.zeros((8, 1), jnp.int32)
        for i in range(8):
            pos = jnp.where(sublane == i, pos_ref[first + i], pos)
        bias_ref[first : first + 8, :] = jnp.where(place <= pos, 0.0, NEG)
    copies[1].wait()
    w_ref[...] = iw_ref[...] * scale
    copies[2].wait()
    copies[3].wait()
    core = lax.axis_index("heads") & 1
    head_sums(n_rows, n_heads, iq_ref, ik_ref[half_at(1 - core, half), :], w_ref, send_ref)
    copies[4].wait()


def kept_logits_kernel(
    n_rows, n_heads, bias_ref, iq_ref, ik_ref, w_ref, q_hbm, keep_ref, q_ref, sem
):
    copy = pltpu.make_async_copy(q_hbm.at[pl.ds(0, q_ref.shape[0]), :], q_ref, sem)
    copy.start()
    half = keep_ref.shape[1]
    core = lax.axis_index("heads") & 1
    head_sums(n_rows, n_heads, iq_ref, ik_ref[half_at(core, half), :], w_ref, keep_ref)
    keep_ref[...] += bias_ref[:, half_at(core, half)]
    copy.wait()


def scores_kernel(
    n_rows, n_heads, bias_ref, q_ref, q_hbm, lat_ref, p_ref, stat_ref, s_even, s_odd, q_rest, sem
):
    ready = q_ref.shape[0]
    copy = pltpu.make_async_copy(q_hbm.at[pl.ds(ready, q_rest.shape[0]), :], q_rest, sem)
    copy.start()
    block = s_even.shape[0]
    blocks = n_rows * n_heads // block

    def dots(b):
        held = s_even if b % 2 == 0 else s_odd
        first = b * block
        if first == ready:
            copy.wait()
        source = q_ref[first : first + block, :] if first < ready else q_rest[
            first - ready : first - ready + block, :
        ]
        held[...] = jnp.dot(source, lat_ref[...], preferred_element_type=F32)

    for b in range(blocks):
        dots(b)
        held = s_even if b % 2 == 0 else s_odd
        for i in range(block // n_heads):
            row = b * (block // n_heads) + i
            x = held[i * n_heads : (i + 1) * n_heads, :] + bias_ref[row : row + 1, :]
            top = jnp.max(x, axis=1, keepdims=True)
            e = jnp.exp2((x - top) * SCORE_LOG2)
            p_ref[row * n_heads : (row + 1) * n_heads, :] = e
            stat_ref[:, row : row + 1] = top
            stat_ref[:, n_rows + row : n_rows + row + 1] = jnp.sum(e, axis=1, keepdims=True)


def index_stats_kernel(mine_ref, other_ref, stat_ref, e_ref, out_ref, col):
    n_rows = mine_ref.shape[0]
    x = (mine_ref[...] + other_ref[...]) * LOG2E
    top = jnp.max(x, axis=1, keepdims=True)
    e = jnp.exp2(x - top)
    e_ref[...] = e
    col[:n_rows, 0:1] = top
    col[n_rows:, 0:1] = jnp.sum(e, axis=1, keepdims=True)
    n = stat_ref.shape[0] // 2
    size = stat_ref[:, :n_rows] * SCORE_LOG2 + jnp.log2(stat_ref[:, n_rows:])
    out_ref[:n, :n_rows] = size[:n, :]
    out_ref[:n, n_rows:] = size[n:, :]
    out_ref[n:, :] = jnp.transpose(col[...])[: out_ref.shape[0] - n, :]


def joined(stats):
    n = stats[0].shape[1] // 2
    tops = [s[:, :n] for s in stats]
    top = functools.reduce(jnp.maximum, tops)
    total = sum(s[:, n:] * jnp.exp2(t - top) for s, t in zip(stats, tops))
    return top, total


def target_sums(n_rows, n_heads, p_ref, weight, at, out_ref):
    for row in range(n_rows):
        out_ref[row : row + 1, :] = jnp.sum(
            p_ref[row * n_heads : (row + 1) * n_heads, at] * weight[:, row : row + 1],
            axis=0,
            keepdims=True,
        )


def target_kernel(n_rows, n_heads, all_ref, own_ref, p_ref, send_ref, weight_ref):
    half = send_ref.shape[1]
    n = all_ref.shape[0]
    some = n_heads // 2
    sizes = [all_ref[k, :some, :] for k in range(n)]
    top = functools.reduce(jnp.maximum, sizes)
    total = sum(jnp.exp2(s - top) for s in sizes)
    tops = own_ref[:, :n_rows] * SCORE_LOG2
    weight = jnp.concatenate(
        [
            jnp.exp2(tops[:some, :] - top[:, :n_rows]) / total[:, :n_rows],
            jnp.exp2(tops[some:, :] - top[:, n_rows:]) / total[:, n_rows:],
        ],
        axis=0,
    )
    peak, mass = joined([all_ref[k, some:, :] for k in range(n)])
    weight_ref[:n_heads, :n_rows] = weight
    for ref, first in ((weight_ref, n_heads), (send_ref, n_rows)):
        ref[first:, :n_rows] = peak
        ref[first:, n_rows : 2 * n_rows] = mass
    core = lax.axis_index("heads") & 1
    target_sums(n_rows, n_heads, p_ref, weight, half_at(1 - core, half), send_ref)


def kept_target_kernel(n_rows, n_heads, weight_ref, p_ref, keep_ref):
    core = lax.axis_index("heads") & 1
    at = half_at(core, keep_ref.shape[1])
    target_sums(n_rows, n_heads, p_ref, weight_ref[:n_heads, :n_rows], at, keep_ref)


def probs_kernel(mine_ref, other_ref, own_ref, e_ref, prob_ref, col):
    n_rows = e_ref.shape[0]
    first = mine_ref.shape[0] - 8
    peak, mass = joined([mine_ref[first:, :], other_ref[n_rows:, : 2 * n_rows]])
    factor = jnp.exp2(own_ref[own_ref.shape[0] - 8 :, :n_rows] - peak) / mass
    col[:8, :n_rows] = factor
    prob_ref[...] = e_ref[...] * jnp.transpose(col[...])[:n_rows, 0:1]


def mask_kernel(iq_ref, ik_ref, w_ref, wm_ref, iqt_ref):
    rows = 256
    n_heads = w_ref.shape[0]
    for b in range(iq_ref.shape[0] // rows):
        at = slice(b * rows, (b + 1) * rows)
        dots = lax.dot_general(iq_ref[at, :], ik_ref[...], CONTRACT_LAST, preferred_element_type=F32)
        for i in range(rows // n_heads):
            row, part = b * (rows // n_heads) + i, slice(i * n_heads, (i + 1) * n_heads)
            wm_ref[b * rows + i * n_heads : b * rows + (i + 1) * n_heads, :] = jnp.where(
                dots[part, :] > 0.0, w_ref[:, row : row + 1], 0.0
            )
        iqt_ref[:, at] = jnp.transpose(iq_ref[at, :])


def coefficients(n_heads, g_rows, wm):
    n = g_rows.shape[1]
    g = jnp.concatenate(
        [jnp.broadcast_to(g_rows[i : i + 1, :], (n_heads, n)) for i in range(g_rows.shape[0])], axis=0
    )
    return (g * wm).astype(BF16)


def own_grads_kernel(n_heads, g_ref, wm_ref, iqt_ref, ik_ref, gq_ref, gkt_ref):
    half = g_ref.shape[1]
    at = half_at(lax.axis_index("heads") & 1, half)
    rows = 256
    per = rows // n_heads
    for b in range(wm_ref.shape[0] // rows):
        row = slice(b * rows, (b + 1) * rows)
        coef = coefficients(n_heads, g_ref[b * per : (b + 1) * per, :], wm_ref[row, at])
        gq_ref[row, :] = jnp.dot(coef, ik_ref[at, :], preferred_element_type=F32)
        term = jnp.dot(iqt_ref[:, row], coef, preferred_element_type=F32)
        if b == 0:
            gkt_ref[...] = term
        else:
            gkt_ref[...] += term


def other_grads_kernel(n_heads, k, g_ref, wm_ref, iqt_ref, ik_ref, gq_ref, *rest):
    *acc_ref, out_ref, gkt_ref = rest
    half = g_ref.shape[1]
    at = half_at(1 - (lax.axis_index("heads") & 1), half)
    rows = out_ref.shape[0]
    per = rows // n_heads
    block = (lax.axis_index("ctx") & (QUAD - 1)) ^ k
    row = pl.ds(pl.multiple_of(block * rows, rows), rows)
    coef = coefficients(
        n_heads, g_ref[pl.ds(pl.multiple_of(block * per, per), per), :], wm_ref[row, at]
    )
    out_ref[...] = gq_ref[row, :] + jnp.dot(coef, ik_ref[at, :], preferred_element_type=F32)
    term = jnp.dot(iqt_ref[:, row], coef, preferred_element_type=F32)
    gkt_ref[...] = acc_ref[0][...] + term if acc_ref else term


def key_grads_kernel(mine_ref, other_ref, *rest):
    *gk_refs, gk_t = rest
    half = mine_ref.shape[1]
    me = lax.axis_index("heads")
    gk_t[:, half_at(me & 1, half)] = mine_ref[...]
    gk_t[:, half_at(1 - (me & 1), half)] = other_ref[...]
    size = gk_refs[0].shape[0]
    for k, ref in enumerate(gk_refs):
        at = pl.multiple_of((me ^ k) * size, LANES)
        ref[...] = jnp.transpose(gk_t[:, pl.ds(at, size)])


def outputs_kernel(n_quad, *refs):
    *in_refs, gq_hbm, gk_hbm, total, sems = refs
    blocks, parts = in_refs[:n_quad], in_refs[n_quad:]
    size = blocks[0].shape[0]
    slot = lax.axis_index("ctx") & (n_quad - 1)
    copies = [
        pltpu.make_async_copy(
            ref, gq_hbm.at[pl.ds(pl.multiple_of((slot ^ k) * size, size), size), :], sems.at[k]
        )
        for k, ref in enumerate(blocks)
    ]
    for copy in copies:
        copy.start()
    total[...] = sum(ref[...] for ref in parts)
    last = pltpu.make_async_copy(total, gk_hbm, sems.at[n_quad])
    last.start()
    for copy in copies + [last]:
        copy.wait()


def body(queries, latents, index_queries, index_keys, index_weights, positions):
    n_rows, heads_local, width = queries.shape
    keys = latents.shape[0]
    index_local, depth = index_queries.shape[1:]
    n_ctx = lax.axis_size("ctx")
    n_heads = lax.axis_size("heads")
    half = keys // 2
    loss_scale = float(n_ctx * keys // 64)
    shape = jax.ShapeDtypeStruct

    def swapped(value, axis, k):
        n = lax.axis_size(axis)
        return lax.ppermute(value, axis, [(i, i ^ k) for i in range(n)])

    flat = (n_rows * index_local, depth)
    send, bias, iq, ik, w, lat = call(
        functools.partial(
            logits_kernel, n_rows, index_local, (index_local * n_heads * depth) ** (-0.5)
        ),
        (
            shape((n_rows, half), F32),
            shape((n_rows, keys), F32),
            shape(flat, BF16),
            shape((keys, depth), BF16),
            shape((index_local, n_rows), F32),
            shape((width, keys), BF16),
        ),
        [HBM] * 5,
        scratch=[
            pltpu.VMEM((index_local, n_rows), F32),
            pltpu.SMEM((n_rows,), jnp.int32),
            pltpu.SemaphoreType.DMA((5,)),
        ],
        flops=flat[0] * depth * keys,
        nbytes=latents.size * 2,
    )(
        *(
            pltpu.with_memory_space_constraint(x, pltpu.HBM)
            for x in (
                positions,
                index_queries.reshape(flat),
                index_keys,
                index_weights.T,
                latents.T,
            )
        )
    )
    got = swapped(send, "heads", 1)
    flat_queries = pltpu.with_memory_space_constraint(
        queries.reshape(n_rows * heads_local, width), pltpu.HBM
    )
    ready = n_rows * heads_local // 8 * 3
    keep, q = call(
        functools.partial(kept_logits_kernel, n_rows, index_local),
        (shape((n_rows, half), F32), shape((ready, width), BF16)),
        [VMEM] * 4 + [HBM],
        scratch=[pltpu.SemaphoreType.DMA],
        flops=flat[0] * depth * keys,
        nbytes=queries.size * 2,
    )(bias, iq, ik, w, flat_queries)
    logit_mine = keep + got
    logit_other = swapped(logit_mine, "heads", 2)
    probs, stats = call(
        functools.partial(scores_kernel, n_rows, heads_local),
        (shape((n_rows * heads_local, keys), F32), shape((heads_local, 2 * n_rows), F32)),
        [VMEM, VMEM, HBM, VMEM],
        scratch=[pltpu.VMEM((256, keys), F32)] * 2
        + [pltpu.VMEM((n_rows * heads_local - ready, width), BF16), pltpu.SemaphoreType.DMA],
        flops=2 * queries.size * keys,
        exps=n_rows * heads_local * keys,
        nbytes=queries.size * 2,
    )(bias, q, flat_queries, lat)
    exps, sizes = call(
        index_stats_kernel,
        (shape((n_rows, half), F32), shape((heads_local // 2 + 8, 2 * n_rows), F32)),
        [VMEM] * 3,
        scratch=[pltpu.VMEM((LANES, LANES), F32)],
    )(logit_mine, logit_other, stats)
    everyone = lax.all_to_all(jnp.broadcast_to(sizes, (n_ctx,) + sizes.shape), "ctx", 0, 0)
    send, weight = call(
        functools.partial(target_kernel, n_rows, heads_local),
        (shape((n_rows + 8, half), F32), shape((heads_local + 8, 2 * n_rows), F32)),
        [VMEM] * 3,
        flops=n_rows * heads_local * keys,
    )(everyone, stats, probs)
    got = swapped(send, "heads", 1)
    keep = call(
        functools.partial(kept_target_kernel, n_rows, heads_local),
        shape((n_rows, half), F32),
        [VMEM] * 2,
        flops=n_rows * heads_local * keys,
    )(weight, probs)
    index_probs = call(
        probs_kernel,
        shape((n_rows, half), F32),
        [VMEM] * 4,
        scratch=[pltpu.VMEM((LANES, LANES), F32)],
    )(weight, got, sizes, exps)
    target = keep + got[:n_rows]
    masked, iq_t = call(
        mask_kernel,
        (shape((flat[0], keys), F32), shape(flat[::-1], BF16)),
        [VMEM] * 3,
        flops=2 * flat[0] * depth * keys,
    )(iq, ik, w)
    rest, masked, iq_t = lax.optimization_barrier((swapped(target, "heads", 2), masked, iq_t))
    target = target + rest
    grad = loss_scale * (index_probs - target * (1.0 / (heads_local * n_heads)))
    grad_other = swapped(grad, "heads", 1)
    query_sums, key_sums = call(
        functools.partial(own_grads_kernel, index_local),
        (shape(flat, F32), shape((depth, half), F32)),
        [VMEM] * 4,
        flops=2 * flat[0] * depth * keys,
    )(grad, masked, iq_t, ik)
    query_parts = [None] * QUAD
    sums = ()
    for k in range(QUAD - 1, -1, -1):
        query_parts[k], more = call(
            functools.partial(other_grads_kernel, index_local, k),
            (shape((flat[0] // QUAD, depth), F32), shape((depth, half), F32)),
            [VMEM] * (5 + len(sums)),
            flops=2 * flat[0] * depth * keys // QUAD,
        )(grad_other, masked, iq_t, ik, query_sums, *sums)
        sums = (more,)
        if k:
            query_parts[k] = swapped(query_parts[k], "ctx", k)
    owned = keys // n_heads
    key_parts = call(
        key_grads_kernel,
        (shape((owned, depth), F32),) * n_heads,
        [VMEM] * 2,
        scratch=[pltpu.VMEM((depth, keys), F32)],
    )(key_sums, *sums)
    mine = sum(query_parts)
    key_parts = [key_parts[0]] + [swapped(key_parts[k], "heads", k) for k in range(1, n_heads)]
    k = QUAD
    while k < n_ctx:
        mine = mine + swapped(mine, "ctx", k)
        k *= 2
    blocks = [mine]
    for k in range(1, QUAD):
        blocks.append(swapped(mine, "ctx", k))
    grad_queries, grad_keys = call(
        functools.partial(outputs_kernel, QUAD),
        (shape(flat, F32), shape((owned, depth), F32)),
        [VMEM] * (QUAD + n_heads),
        out_specs=(HBM, HBM),
        scratch=[pltpu.VMEM((owned, depth), F32), pltpu.SemaphoreType.DMA((QUAD + 1,))],
    )(*blocks, *key_parts)
    return grad_queries.reshape(n_rows, index_local, depth), grad_keys


def solution(mesh):
    placed = (
        P(None, "heads", None),
        P("ctx", None),
        P(None, "heads", None),
        P("ctx", None),
        P(None, "heads"),
        P(),
    )
    return jax.shard_map(
        body,
        mesh=mesh,
        in_specs=placed,
        out_specs=(P(None, "heads", None), P(("ctx", "heads"), None)),
        check_vma=False,
    )
```

```python
import functools
import math

import jax
import jax.numpy as jnp
from jax import lax
from jax.experimental import pallas as pl
from jax.experimental.pallas import tpu as pltpu
from jax.sharding import PartitionSpec as P


F32 = jnp.float32
BF16 = jnp.bfloat16
LOG2E = math.log2(math.e)
SCORE_LOG2 = 192 ** (-0.5) * LOG2E
NEG = -1e30
LANES = 128
VMEM = pl.BlockSpec(memory_space=pltpu.VMEM)
HBM = pl.BlockSpec(memory_space=pltpu.HBM)
CONTRACT_LAST = (((1,), (1,)), ((), ()))
SENT = (1, 3, 2, 0)
QUAD = 4


def call(kernel, out_shape, in_specs, out_specs=None, scratch=(), flops=0, exps=0, nbytes=0, aliases=None):
    if out_specs is None:
        out_specs = jax.tree.map(lambda s: VMEM, out_shape)
    return pl.pallas_call(
        kernel,
        out_shape=out_shape,
        in_specs=in_specs,
        out_specs=out_specs,
        scratch_shapes=list(scratch),
        input_output_aliases=aliases or {},
        compiler_params=pltpu.CompilerParams(vmem_limit_bytes=40 << 20),
        cost_estimate=pl.CostEstimate(flops=flops, transcendentals=exps, bytes_accessed=nbytes),
    )


def half_at(core, half):
    return pl.ds(pl.multiple_of(core * half, LANES), half)


def head_sums(n_rows, n_heads, iq_ref, keys, w_ref, out_ref):
    rows = 256
    per = rows // n_heads
    for b in range(n_rows * n_heads // rows):
        dots = lax.dot_general(
            iq_ref[b * rows : (b + 1) * rows, :], keys, CONTRACT_LAST, preferred_element_type=F32
        )
        for i in range(per):
            row = b * per + i
            at = slice(row * n_heads, (row + 1) * n_heads)
            out_ref[row : row + 1, :] = jnp.sum(
                jnp.maximum(dots[i * n_heads : (i + 1) * n_heads, :], 0.0) * w_ref[at, 0:1],
                axis=0,
                keepdims=True,
            )


def logits_kernel(
    n_rows, n_heads, scale,
    pos_hbm, iq_hbm, ik_hbm, iw_hbm, lat_hbm,
    send_ref, bias_ref, iq_ref, ik_ref, w_ref, lat_ref,
    iw_ref, pos_ref, sems,
):
    half = send_ref.shape[1]
    copies = [
        pltpu.make_async_copy(a, b, sems.at[i])
        for i, (a, b) in enumerate(
            (
                (pos_hbm, pos_ref),
                (iw_hbm, iw_ref),
                (ik_hbm, ik_ref),
                (iq_hbm, iq_ref),
                (lat_hbm, lat_ref),
            )
        )
    ]
    for copy in copies:
        copy.start()
    copies[0].wait()
    place = lax.axis_index("ctx") * 2 * half + lax.broadcasted_iota(jnp.int32, (8, 2 * half), 1)
    sublane = lax.broadcasted_iota(jnp.int32, (8, 1), 0)
    for first in range(0, n_rows, 8):
        pos = jnp.zeros((8, 1), jnp.int32)
        for i in range(8):
            pos = jnp.where(sublane == i, pos_ref[first + i], pos)
        bias_ref[first : first + 8, :] = jnp.where(place <= pos, 0.0, NEG)
    copies[1].wait()
    for row in range(n_rows):
        w_ref[row * n_heads : (row + 1) * n_heads, :] = jnp.broadcast_to(
            iw_ref[:, row : row + 1] * scale, (n_heads, LANES)
        )
    copies[2].wait()
    copies[3].wait()
    core = lax.axis_index("heads") & 1
    head_sums(n_rows, n_heads, iq_ref, ik_ref[half_at(1 - core, half), :], w_ref, send_ref)
    copies[4].wait()


def kept_logits_kernel(
    n_rows, n_heads, bias_ref, iq_ref, ik_ref, w_ref, q_hbm, keep_ref, q_ref, sem
):
    copy = pltpu.make_async_copy(q_hbm.at[pl.ds(0, q_ref.shape[0]), :], q_ref, sem)
    copy.start()
    half = keep_ref.shape[1]
    core = lax.axis_index("heads") & 1
    head_sums(n_rows, n_heads, iq_ref, ik_ref[half_at(core, half), :], w_ref, keep_ref)
    keep_ref[...] += bias_ref[:, half_at(core, half)]
    copy.wait()


def scores_kernel(
    n_rows, n_heads, bias_ref, q_ref, q_hbm, lat_ref, p_ref, stat_ref, s_even, s_odd, q_rest, sem
):
    ready = q_ref.shape[0]
    copy = pltpu.make_async_copy(q_hbm.at[pl.ds(ready, q_rest.shape[0]), :], q_rest, sem)
    copy.start()
    block = s_even.shape[0]
    blocks = n_rows * n_heads // block

    def dots(b):
        held = s_even if b % 2 == 0 else s_odd
        first = b * block
        if first == ready:
            copy.wait()
        source = q_ref[first : first + block, :] if first < ready else q_rest[
            first - ready : first - ready + block, :
        ]
        held[...] = jnp.dot(source, lat_ref[...], preferred_element_type=F32)

    dots(0)
    for b in range(blocks):
        if b + 1 < blocks:
            dots(b + 1)
        held = s_even if b % 2 == 0 else s_odd
        for i in range(block // n_heads):
            row = b * (block // n_heads) + i
            x = held[i * n_heads : (i + 1) * n_heads, :] + bias_ref[row : row + 1, :]
            top = jnp.max(x, axis=1, keepdims=True)
            e = jnp.exp2((x - top) * SCORE_LOG2)
            p_ref[row * n_heads : (row + 1) * n_heads, :] = e
            stat_ref[:, row : row + 1] = top
            stat_ref[:, n_rows + row : n_rows + row + 1] = jnp.sum(e, axis=1, keepdims=True)


def index_stats_kernel(mine_ref, other_ref, stat_ref, e_ref, out_ref, col):
    n_rows = mine_ref.shape[0]
    x = (mine_ref[...] + other_ref[...]) * LOG2E
    top = jnp.max(x, axis=1, keepdims=True)
    e = jnp.exp2(x - top)
    e_ref[...] = e
    col[:n_rows, 0:1] = top
    col[n_rows:, 0:1] = jnp.sum(e, axis=1, keepdims=True)
    n = stat_ref.shape[0] // 2
    size = stat_ref[:, :n_rows] * SCORE_LOG2 + jnp.log2(stat_ref[:, n_rows:])
    out_ref[:n, :n_rows] = size[:n, :]
    out_ref[:n, n_rows:] = size[n:, :]
    out_ref[n:, :] = jnp.transpose(col[...])[: out_ref.shape[0] - n, :]


def joined(stats):
    n = stats[0].shape[1] // 2
    tops = [s[:, :n] for s in stats]
    top = functools.reduce(jnp.maximum, tops)
    total = sum(s[:, n:] * jnp.exp2(t - top) for s, t in zip(stats, tops))
    return top, total


def target_sums(n_rows, n_heads, p_ref, weight, at, out_ref):
    for row in range(n_rows):
        out_ref[row : row + 1, :] = jnp.sum(
            p_ref[row * n_heads : (row + 1) * n_heads, at] * weight[:, row : row + 1],
            axis=0,
            keepdims=True,
        )


def target_kernel(n_rows, n_heads, all_ref, own_ref, p_ref, send_ref, weight_ref):
    half = send_ref.shape[1]
    n = all_ref.shape[0]
    some = n_heads // 2
    sizes = [all_ref[k, :some, :] for k in range(n)]
    top = functools.reduce(jnp.maximum, sizes)
    total = sum(jnp.exp2(s - top) for s in sizes)
    tops = own_ref[:, :n_rows] * SCORE_LOG2
    weight = jnp.concatenate(
        [
            jnp.exp2(tops[:some, :] - top[:, :n_rows]) / total[:, :n_rows],
            jnp.exp2(tops[some:, :] - top[:, n_rows:]) / total[:, n_rows:],
        ],
        axis=0,
    )
    peak, mass = joined([all_ref[k, some:, :] for k in range(n)])
    weight_ref[:n_heads, :n_rows] = weight
    for ref, first in ((weight_ref, n_heads), (send_ref, n_rows)):
        ref[first:, :n_rows] = peak
        ref[first:, n_rows : 2 * n_rows] = mass
    core = lax.axis_index("heads") & 1
    target_sums(n_rows, n_heads, p_ref, weight, half_at(1 - core, half), send_ref)


def kept_target_kernel(n_rows, n_heads, weight_ref, p_ref, keep_ref):
    core = lax.axis_index("heads") & 1
    at = half_at(core, keep_ref.shape[1])
    target_sums(n_rows, n_heads, p_ref, weight_ref[:n_heads, :n_rows], at, keep_ref)


def probs_kernel(mine_ref, other_ref, own_ref, e_ref, prob_ref, col):
    n_rows = e_ref.shape[0]
    first = mine_ref.shape[0] - 8
    peak, mass = joined([mine_ref[first:, :], other_ref[n_rows:, : 2 * n_rows]])
    factor = jnp.exp2(own_ref[own_ref.shape[0] - 8 :, :n_rows] - peak) / mass
    col[:8, :n_rows] = factor
    prob_ref[...] = e_ref[...] * jnp.transpose(col[...])[:n_rows, 0:1]


def mask_kernel(iq_ref, ik_ref, w_ref, wm_ref, iqt_ref):
    rows = 256
    for b in range(iq_ref.shape[0] // rows):
        at = slice(b * rows, (b + 1) * rows)
        dots = lax.dot_general(iq_ref[at, :], ik_ref[...], CONTRACT_LAST, preferred_element_type=F32)
        wm_ref[at, :] = jnp.where(dots > 0.0, w_ref[at, 0:1], 0.0)
        iqt_ref[:, at] = jnp.transpose(iq_ref[at, :])


def coefficients(n_heads, g_rows, wm):
    n = g_rows.shape[1]
    g = jnp.concatenate(
        [jnp.broadcast_to(g_rows[i : i + 1, :], (n_heads, n)) for i in range(g_rows.shape[0])], axis=0
    )
    return (g * wm).astype(BF16)


def own_grads_kernel(n_heads, g_ref, wm_ref, iqt_ref, ik_ref, gq_ref, gkt_ref):
    half = g_ref.shape[1]
    at = half_at(lax.axis_index("heads") & 1, half)
    rows = 256
    per = rows // n_heads
    for b in range(wm_ref.shape[0] // rows):
        row = slice(b * rows, (b + 1) * rows)
        coef = coefficients(n_heads, g_ref[b * per : (b + 1) * per, :], wm_ref[row, at])
        gq_ref[row, :] = jnp.dot(coef, ik_ref[at, :], preferred_element_type=F32)
        term = jnp.dot(iqt_ref[:, row], coef, preferred_element_type=F32)
        if b == 0:
            gkt_ref[...] = term
        else:
            gkt_ref[...] += term


def other_grads_kernel(n_heads, k, g_ref, wm_ref, iqt_ref, ik_ref, gq_ref, *rest):
    *acc_ref, out_ref, gkt_ref = rest
    half = g_ref.shape[1]
    at = half_at(1 - (lax.axis_index("heads") & 1), half)
    rows = out_ref.shape[0]
    per = rows // n_heads
    block = (lax.axis_index("ctx") & (QUAD - 1)) ^ k
    row = pl.ds(pl.multiple_of(block * rows, rows), rows)
    coef = coefficients(
        n_heads, g_ref[pl.ds(pl.multiple_of(block * per, per), per), :], wm_ref[row, at]
    )
    out_ref[...] = gq_ref[row, :] + jnp.dot(coef, ik_ref[at, :], preferred_element_type=F32)
    term = jnp.dot(iqt_ref[:, row], coef, preferred_element_type=F32)
    gkt_ref[...] = acc_ref[0][...] + term if acc_ref else term


def key_grads_kernel(mine_ref, other_ref, *rest):
    *gk_refs, gk_t = rest
    half = mine_ref.shape[1]
    me = lax.axis_index("heads")
    gk_t[:, half_at(me & 1, half)] = mine_ref[...]
    gk_t[:, half_at(1 - (me & 1), half)] = other_ref[...]
    size = gk_refs[0].shape[0]
    for k, ref in enumerate(gk_refs):
        at = pl.multiple_of((me ^ k) * size, LANES)
        ref[...] = jnp.transpose(gk_t[:, pl.ds(at, size)])


def place_blocks(first, refs, gq_hbm, sems):
    size = refs[0].shape[0]
    slot = lax.axis_index("ctx") & (QUAD - 1)
    copies = []
    for i, ref in enumerate(refs):
        at = pl.multiple_of((slot ^ (first + i)) * size, size)
        copies.append(pltpu.make_async_copy(ref, gq_hbm.at[pl.ds(at, size), :], sems.at[i]))
        copies[-1].start()
    return copies


def early_outputs_kernel(mine_ref, *rest):
    *parts, gq_hbm, gk_hbm, total, sems = rest
    copies = place_blocks(0, [mine_ref], gq_hbm, sems)
    total[...] = sum(ref[...] for ref in parts)
    copies.append(pltpu.make_async_copy(total, gk_hbm, sems.at[1]))
    copies[-1].start()
    for copy in copies:
        copy.wait()


def late_outputs_kernel(begun_hbm, *rest):
    *blocks, gq_hbm, sems = rest
    for copy in place_blocks(1, blocks, gq_hbm, sems):
        copy.wait()


def body(queries, latents, index_queries, index_keys, index_weights, positions):
    n_rows, heads_local, width = queries.shape
    keys = latents.shape[0]
    index_local, depth = index_queries.shape[1:]
    n_ctx = lax.axis_size("ctx")
    n_heads = lax.axis_size("heads")
    half = keys // 2
    loss_scale = float(n_ctx * keys // 64)
    shape = jax.ShapeDtypeStruct

    def swapped(value, axis, k):
        n = lax.axis_size(axis)
        return lax.ppermute(value, axis, [(i, i ^ k) for i in range(n)])

    flat = (n_rows * index_local, depth)
    send, bias, iq, ik, w, lat = call(
        functools.partial(
            logits_kernel, n_rows, index_local, (index_local * n_heads * depth) ** (-0.5)
        ),
        (
            shape((n_rows, half), F32),
            shape((n_rows, keys), F32),
            shape(flat, BF16),
            shape((keys, depth), BF16),
            shape((flat[0], LANES), F32),
            shape((width, keys), BF16),
        ),
        [HBM] * 5,
        scratch=[
            pltpu.VMEM((index_local, n_rows), F32),
            pltpu.SMEM((n_rows,), jnp.int32),
            pltpu.SemaphoreType.DMA((5,)),
        ],
        flops=flat[0] * depth * keys,
        nbytes=latents.size * 2,
    )(
        *(
            pltpu.with_memory_space_constraint(x, pltpu.HBM)
            for x in (
                positions,
                index_queries.reshape(flat),
                index_keys,
                index_weights.T,
                latents.T,
            )
        )
    )
    got = swapped(send, "heads", 1)
    flat_queries = pltpu.with_memory_space_constraint(
        queries.reshape(n_rows * heads_local, width), pltpu.HBM
    )
    ready = n_rows * heads_local // 2
    keep, q = call(
        functools.partial(kept_logits_kernel, n_rows, index_local),
        (shape((n_rows, half), F32), shape((ready, width), BF16)),
        [VMEM] * 4 + [HBM],
        scratch=[pltpu.SemaphoreType.DMA],
        flops=flat[0] * depth * keys,
        nbytes=queries.size * 2,
    )(bias, iq, ik, w, flat_queries)
    logit_mine = keep + got
    logit_other = swapped(logit_mine, "heads", 2)
    probs, stats = call(
        functools.partial(scores_kernel, n_rows, heads_local),
        (shape((n_rows * heads_local, keys), F32), shape((heads_local, 2 * n_rows), F32)),
        [VMEM, VMEM, HBM, VMEM],
        scratch=[pltpu.VMEM((256, keys), F32)] * 2
        + [pltpu.VMEM((n_rows * heads_local - ready, width), BF16), pltpu.SemaphoreType.DMA],
        flops=2 * queries.size * keys,
        exps=n_rows * heads_local * keys,
        nbytes=queries.size * 2,
    )(bias, q, flat_queries, lat)
    exps, sizes = call(
        index_stats_kernel,
        (shape((n_rows, half), F32), shape((heads_local // 2 + 8, 2 * n_rows), F32)),
        [VMEM] * 3,
        scratch=[pltpu.VMEM((LANES, LANES), F32)],
    )(logit_mine, logit_other, stats)
    everyone = lax.all_to_all(jnp.broadcast_to(sizes, (n_ctx,) + sizes.shape), "ctx", 0, 0)
    send, weight = call(
        functools.partial(target_kernel, n_rows, heads_local),
        (shape((n_rows + 8, half), F32), shape((heads_local + 8, 2 * n_rows), F32)),
        [VMEM] * 3,
        flops=n_rows * heads_local * keys,
    )(everyone, stats, probs)
    got = swapped(send, "heads", 1)
    keep = call(
        functools.partial(kept_target_kernel, n_rows, heads_local),
        shape((n_rows, half), F32),
        [VMEM] * 2,
        flops=n_rows * heads_local * keys,
    )(weight, probs)
    index_probs = call(
        probs_kernel,
        shape((n_rows, half), F32),
        [VMEM] * 4,
        scratch=[pltpu.VMEM((LANES, LANES), F32)],
    )(weight, got, sizes, exps)
    target = keep + got[:n_rows]
    masked, iq_t = call(
        mask_kernel,
        (shape((flat[0], keys), F32), shape(flat[::-1], BF16)),
        [VMEM] * 3,
        flops=2 * flat[0] * depth * keys,
    )(iq, ik, w)
    rest, masked, iq_t = lax.optimization_barrier((swapped(target, "heads", 2), masked, iq_t))
    target = target + rest
    grad = loss_scale * (index_probs - target * (1.0 / (heads_local * n_heads)))
    grad_other = swapped(grad, "heads", 1)
    query_sums, key_sums = call(
        functools.partial(own_grads_kernel, index_local),
        (shape(flat, F32), shape((depth, half), F32)),
        [VMEM] * 4,
        flops=2 * flat[0] * depth * keys,
    )(grad, masked, iq_t, ik)
    query_parts = [None] * QUAD
    sums = ()
    for k in SENT:
        query_parts[k], more = call(
            functools.partial(other_grads_kernel, index_local, k),
            (shape((flat[0] // QUAD, depth), F32), shape((depth, half), F32)),
            [VMEM] * (5 + len(sums)),
            flops=2 * flat[0] * depth * keys // QUAD,
        )(grad_other, masked, iq_t, ik, query_sums, *sums)
        sums = (more,)
        if k:
            query_parts[k] = swapped(query_parts[k], "ctx", k)
    owned = keys // n_heads
    key_parts = call(
        key_grads_kernel,
        (shape((owned, depth), F32),) * n_heads,
        [VMEM] * 2,
        scratch=[pltpu.VMEM((depth, keys), F32)],
    )(key_sums, *sums)
    mine = sum(query_parts)
    key_parts = [key_parts[0]] + [swapped(key_parts[k], "heads", k) for k in range(1, n_heads)]
    k = QUAD
    while k < n_ctx:
        mine = mine + swapped(mine, "ctx", k)
        k *= 2
    blocks = [mine]
    for k in range(1, QUAD):
        blocks.append(swapped(mine, "ctx", k))
    begun, grad_keys = call(
        early_outputs_kernel,
        (shape(flat, F32), shape((owned, depth), F32)),
        [VMEM] * (1 + n_heads),
        out_specs=(HBM, HBM),
        scratch=[pltpu.VMEM((owned, depth), F32), pltpu.SemaphoreType.DMA((2,))],
    )(mine, *key_parts)
    grad_queries = call(
        late_outputs_kernel,
        shape(flat, F32),
        [HBM] + [VMEM] * (QUAD - 1),
        out_specs=HBM,
        scratch=[pltpu.SemaphoreType.DMA((QUAD - 1,))],
        aliases={0: 0},
    )(begun, *blocks[1:])
    return grad_queries.reshape(n_rows, index_local, depth), grad_keys


def solution(mesh):
    placed = (
        P(None, "heads", None),
        P("ctx", None),
        P(None, "heads", None),
        P("ctx", None),
        P(None, "heads"),
        P(),
    )
    return jax.shard_map(
        body,
        mesh=mesh,
        in_specs=placed,
        out_specs=(P(None, "heads", None), P(("ctx", "heads"), None)),
        check_vma=False,
    )
```
